512 devices in a mesh: flow: 8 (over y), cross: 64 (over x, z, core).
Axes of the slice: x: 4, y: 8, z: 8, core: 2. Of those that a mesh axis runs over, the one named last changes fastest.
Arguments:
- conc_old: float32 [8, 64, 64, 8, 128], P('flow', 'cross'), may hold values from 0.05 to 2
- face_flux: float32 [8, 64, 8, 128, 128], P('flow', 'cross'), may hold values from 0 to 0.01484375
- block_inverse: float32 [8, 64, 8, 128, 128], P('flow', 'cross'), may hold values from 0 to 1
- upstream_block: int32 [8, 64, 8], P('flow', 'cross'), may hold values from 0 to 6, as said below
- send_cells: int32 [8, 64, 64, 128], P('flow', 'cross'), may hold values from 0 to 1023
- send_count: int32 [8, 64, 64], P('flow', 'cross'), may hold values from 0 to 128, as said below
- recv_cells: int32 [8, 64, 64, 128], P('flow', 'cross'), may hold values from 0 to 1023
- recv_coef: float32 [8, 64, 64, 128], P('flow', 'cross'), may hold values from 0.1 to 1
Outputs:
- conc_new: float32 [8, 64, 64, 8, 128], P('flow', 'cross')
The draws below stay inside these ranges and needn't reach their ends.
Inputs may be any that keep to these rules, and one draw needn't show every extreme that they name: For j >= 1, upstream_block[f, q, j] < j; entry 0 is unused and is 0; block 7 is fed by block 6. `send_count`: entry [f, s, d] counts the live slots from device s to device d of the cross axis; a device sends nothing to itself; every device sends a full 128 to at least one other device and receives a full 128 from at least one.
All inputs are finite; a program needn't handle non-finite values.
Results may differ from the reference program's by a relative error of at most 0.0003.
Values sent between devices are 32-bit elements; how exact they have to be, the bound alone decides.
A program may use at most 64 MiB of HBM per device.

```python
import math
import jax
import jax.numpy as jnp
from jax import lax

E = 64
B = 128
NB = 8
SLOTS = 128
N_FLOW = 8
N_CROSS = 64


def draw_upstream_block(key, part):
    shape = (N_FLOW, N_CROSS, NB)
    raw_draw = jax.random.randint(jax.random.fold_in(key, 11), shape, 0, 1 << 20)
    block_id = lax.broadcasted_iota(jnp.int32, shape, 2)
    picked = raw_draw % jnp.maximum(block_id, 1)
    return jnp.where(block_id == NB - 1, NB - 2, picked).astype(jnp.int32)


def draw_send_count(key, part):
    shape = (N_FLOW, N_CROSS, N_CROSS)
    base_count = jax.random.randint(jax.random.fold_in(key, 21), shape, SLOTS // 2, SLOTS + 1)
    offset = jax.random.randint(jax.random.fold_in(key, 22), (N_FLOW, 1, 1), 1, N_CROSS)
    sender = lax.broadcasted_iota(jnp.int32, shape, 1)
    target = lax.broadcasted_iota(jnp.int32, shape, 2)
    full_slot = target == (sender + offset) % N_CROSS
    counted = jnp.where(full_slot, SLOTS, base_count)
    return jnp.where(sender == target, 0, counted).astype(jnp.int32)


def draw_block_inverse(key, part):
    shape = (N_FLOW, N_CROSS, NB, B, B)
    diagonal = jax.random.uniform(jax.random.fold_in(key, 31), shape[:-1], jnp.float32, 0.4, 0.7)
    spread = jax.random.uniform(jax.random.fold_in(key, 32), shape, jnp.float32, 0.0, 0.6 / B)
    rows = lax.broadcasted_iota(jnp.int32, shape, 3)
    columns = lax.broadcasted_iota(jnp.int32, shape, 4)
    unit = (rows == columns).astype(jnp.float32)
    return (spread + unit * diagonal[..., None]).astype(jnp.float32)


def plant(entries, stream_key, smallest, top_value):
    longest = entries.shape.index(max(entries.shape))
    spots = []
    for shift in (0, 1):
        where = [jax.random.randint(jax.random.fold_in(stream_key, axis), (), 0, length) for axis, length in enumerate(entries.shape)]
        where[longest] = (where[longest] + shift) % entries.shape[longest]
        spots.append(tuple(where))
    return entries.at[spots[0]].set(smallest).at[spots[1]].set(top_value)


def steps_of(own_key, extent, pieces, low, top_value):
    loudness, own = 1.0, jax.random.fold_in(own_key, 6)
    for dim, parts in pieces:
        steps = jnp.exp(jax.random.uniform(jax.random.fold_in(own, dim), (parts,), jnp.float32, low / len(pieces), top_value / len(pieces)))
        loudness = loudness * jnp.repeat(steps, extent[dim] // parts).reshape([-1 if axis == dim else 1 for axis in range(len(extent))])
    return loudness


def setup_inputs(seed: int = 0) -> dict:
    arg_keys = jax.random.split(jax.random.key(seed), 9)
    conc_old = jnp.clip(jnp.exp(math.log(2.0) - 3.6888794 * jax.random.uniform(arg_keys[0], (N_FLOW, N_CROSS, E, NB, B), jnp.float32) ** steps_of(arg_keys[0], (N_FLOW, N_CROSS, E, NB, B), ((0, 8), (1, 64)), -0.2, 0.2)), 0.05, 2.0)
    face_flux = jnp.clip(0.01484375 * jax.random.uniform(arg_keys[1], (N_FLOW, N_CROSS, NB, B, B), jnp.float32) ** steps_of(arg_keys[1], (N_FLOW, N_CROSS, NB, B, B), ((0, 8), (1, 64)), -0.2, 0.2), 0.0, 0.01484375)
    block_inverse = draw_block_inverse(jax.random.fold_in(arg_keys[8], 71), 0)
    upstream_block = draw_upstream_block(jax.random.fold_in(arg_keys[8], 71), 0)
    send_cells = plant(jax.random.randint(arg_keys[4], (N_FLOW, N_CROSS, N_CROSS, SLOTS), 0, NB * B), jax.random.fold_in(arg_keys[4], 1), 0, (NB * B) - 1).astype(jnp.int32)
    send_count = draw_send_count(jax.random.fold_in(arg_keys[8], 71), 0)
    recv_cells = plant(jax.random.randint(arg_keys[6], (N_FLOW, N_CROSS, N_CROSS, SLOTS), 0, NB * B), jax.random.fold_in(arg_keys[6], 1), 0, (NB * B) - 1).astype(jnp.int32)
    recv_coef = jnp.clip(jnp.exp(math.log(1.0) - 2.3025851 * jax.random.uniform(arg_keys[7], (N_FLOW, N_CROSS, N_CROSS, SLOTS), jnp.float32) ** steps_of(arg_keys[7], (N_FLOW, N_CROSS, N_CROSS, SLOTS), ((0, 8), (1, 64)), -0.2, 0.2)), 0.1, 1.0)
    return dict(conc_old=conc_old, face_flux=face_flux, block_inverse=block_inverse, upstream_block=upstream_block, send_cells=send_cells, send_count=send_count, recv_cells=recv_cells, recv_coef=recv_coef)


def matmul(left, right):
    return jnp.dot(left, right, precision=lax.Precision.HIGHEST, preferred_element_type=jnp.float32)


def upwind_sweep(incoming, source, couplings, inverses, feeders):
    blocks = source.shape[1]
    head_block = matmul(source[:, 0] + matmul(incoming, couplings[0]), inverses[0])
    solved_all = jnp.zeros_like(source).at[:, 0].set(head_block)

    def advance(block_id, solved_all):
        block_id = block_id.astype(jnp.int32)
        feeder = lax.dynamic_index_in_dim(solved_all, feeders[block_id].astype(jnp.int32), 1, keepdims=False)
        block_source = lax.dynamic_index_in_dim(source, block_id, 1, keepdims=False)
        coupling = lax.dynamic_index_in_dim(couplings, block_id, 0, keepdims=False)
        inverse = lax.dynamic_index_in_dim(inverses, block_id, 0, keepdims=False)
        solved = matmul(block_source + matmul(feeder, coupling), inverse)
        return lax.dynamic_update_index_in_dim(solved_all, solved, block_id, 1)

    return lax.fori_loop(1, blocks, advance, solved_all)


def lateral_inflow(current, send_cells, send_count, recv_cells, recv_coef):
    n_cross, members = current.shape[0], current.shape[1]
    flat_conc = current.reshape(n_cross, members, -1)
    slot_count = send_cells.shape[-1]
    picked = jax.vmap(lambda conc_one, cells_one: conc_one[:, cells_one.reshape(-1)])(flat_conc, send_cells)
    picked = picked.reshape(n_cross, members, n_cross, slot_count)
    live_slot = lax.broadcasted_iota(jnp.int32, (n_cross, n_cross, slot_count), 2) < send_count[:, :, None]
    outgoing = jnp.where(live_slot[:, None], picked, 0.0)

    def deposit(receiver):
        arrived = jnp.transpose(lax.dynamic_index_in_dim(outgoing, receiver, 2, keepdims=False), (1, 0, 2))
        weighted = arrived * recv_coef[receiver][None]
        empty = jnp.zeros((members, flat_conc.shape[2]), jnp.float32)
        return empty.at[:, recv_cells[receiver].reshape(-1)].add(weighted.reshape(members, -1))

    return lax.map(deposit, jnp.arange(n_cross, dtype=jnp.int32)).reshape(current.shape)


def reference(conc_old, face_flux, block_inverse, upstream_block, send_cells, send_count, recv_cells, recv_coef):
    sweeper = jax.vmap(upwind_sweep)
    incoming = jnp.zeros((N_CROSS, E, B), jnp.float32)
    results = []
    for flow_id in range(N_FLOW):
        lateral = lateral_inflow(conc_old[flow_id], send_cells[flow_id], send_count[flow_id], recv_cells[flow_id], recv_coef[flow_id])
        source = conc_old[flow_id] + lateral
        solved = sweeper(incoming, source, face_flux[flow_id], block_inverse[flow_id], upstream_block[flow_id])
        results.append(solved)
        incoming = solved[:, :, -1]
    return jnp.stack(results)
```

```python
import jax
import jax.numpy as jnp
from jax import lax
from jax.experimental import pallas as pl
from jax.experimental.pallas import tpu as pltpu
from jax.sharding import PartitionSpec as P

MESH = pl.DeviceIdType.MESH
E, NB, B = 64, 8, 128
CELLS = NB * B
N_FLOW = 8


def split(value):
    high = value.astype(jnp.bfloat16)
    low = (value - high.astype(jnp.float32)).astype(jnp.bfloat16)
    return high, low


def dot(left, right):
    return jnp.dot(left, right, preferred_element_type=jnp.float32)


def dot3(left, right):
    left_high, left_low = left
    right_high, right_low = right
    return dot(left_high, right_high) + dot(left_low, right_high) + dot(left_high, right_low)


def build_response(feeders, flux_ref, inverse_ref, resp_high, resp_low):
    resp_high[0] = jnp.zeros((CELLS + B, B), jnp.bfloat16)
    resp_low[0] = jnp.zeros((CELLS + B, B), jnp.bfloat16)
    first = split(dot3(split(flux_ref[0]), split(inverse_ref[0])))
    resp_high[0, pl.ds(CELLS, B), :] = first[0]
    resp_low[0, pl.ds(CELLS, B), :] = first[1]
    own = split(inverse_ref[0])
    resp_high[0, pl.ds(0, B), :] = own[0]
    resp_low[0, pl.ds(0, B), :] = own[1]

    def advance(j, carry):
        feeder = feeders[j]
        own = split(inverse_ref[j])
        step = split(dot3(split(flux_ref[j]), own))
        rows = split(dot3((resp_high[feeder], resp_low[feeder]), step))
        resp_high[j] = rows[0]
        resp_low[j] = rows[1]
        spot = pl.ds(pl.multiple_of(j * B, B), B)
        resp_high[j, spot, :] = own[0]
        resp_low[j, spot, :] = own[1]
        return carry

    lax.fori_loop(1, NB, advance, 0)


def sweep_kernel(feeders, source_ref, flux_ref, inverse_ref, out_ref,
                 resp_high, resp_low, src, local, incoming, outlet, send_sem, recv_sem):
    me = lax.axis_index("flow")
    right, left = lax.rem(me + 1, N_FLOW), lax.rem(me + N_FLOW - 1, N_FLOW)
    barrier = pltpu.get_barrier_semaphore()
    for neighbour in (left, right):
        pl.semaphore_signal(barrier, inc=1, device_id={"flow": neighbour}, device_id_type=MESH)
    build_response(feeders, flux_ref, inverse_ref, resp_high, resp_low)
    for b in range(NB):
        high, low = split(source_ref[:, b, :])
        src[pl.ds(0, E), pl.ds(b * B, B)] = high
        src[pl.ds(E, E), pl.ds(b * B, B)] = low

    def solve(j):
        both = dot(src[...], resp_high[j, pl.ds(0, CELLS), :])
        return both[:E] + both[E:] + dot(src[pl.ds(0, E), :], resp_low[j, pl.ds(0, CELLS), :])

    def entering(j, parts):
        return dot3(parts, (resp_high[j, pl.ds(CELLS, B), :], resp_low[j, pl.ds(CELLS, B), :]))

    pl.semaphore_wait(barrier, 2)
    copy = pltpu.make_async_remote_copy(
        src_ref=outlet, dst_ref=incoming, send_sem=send_sem, recv_sem=recv_sem,
        device_id={"flow": right}, device_id_type=MESH)
    last = solve(NB - 1)

    @pl.when(me == 0)
    def _():
        outlet[...] = last
        copy.start()
        incoming[...] = jnp.zeros_like(incoming)

    for j in range(NB - 1):
        local[j] = solve(j)

    @pl.when(me > 0)
    def _():
        copy.wait_recv()
        outlet[...] = last + entering(NB - 1, split(incoming[...]))

        @pl.when(me < N_FLOW - 1)
        def _():
            copy.start()

    out_ref[:, NB - 1, :] = outlet[...]
    parts = split(incoming[...])
    for j in range(NB - 1):
        out_ref[:, j, :] = local[j] + entering(j, parts)

    @pl.when(me < N_FLOW - 1)
    def _():
        copy.wait_send()


def sweep(source, couplings, inverses, feeders):
    vmem = pl.BlockSpec(memory_space=pltpu.VMEM)
    return pl.pallas_call(
        sweep_kernel,
        out_shape=jax.ShapeDtypeStruct((E, NB, B), jnp.float32),
        in_specs=[pl.BlockSpec(memory_space=pltpu.SMEM), vmem, vmem, vmem],
        out_specs=vmem,
        scratch_shapes=[
            pltpu.VMEM((NB, CELLS + B, B), jnp.bfloat16),
            pltpu.VMEM((NB, CELLS + B, B), jnp.bfloat16),
            pltpu.VMEM((2 * E, CELLS), jnp.bfloat16),
            pltpu.VMEM((NB, E, B), jnp.float32),
            pltpu.VMEM((E, B), jnp.float32),
            pltpu.VMEM((E, B), jnp.float32),
            pltpu.SemaphoreType.DMA,
            pltpu.SemaphoreType.DMA,
        ],
        compiler_params=pltpu.CompilerParams(collective_id=0, has_side_effects=True),
        name="sweep",
    )(feeders, source, couplings, inverses)


def on_device(conc_old, face_flux, block_inverse, upstream_block, send_cells, send_count, recv_cells, recv_coef):
    current = conc_old[0, 0]
    members = current.shape[0]
    flat_conc = current.reshape(members, -1)
    n_cross, slot_count = (send_cells.shape[2], send_cells.shape[3])
    send_index = send_cells[0, 0].reshape(-1)
    picked = flat_conc[:, send_index].reshape(members, n_cross, slot_count)
    live_slot = (
        lax.broadcasted_iota(jnp.int32, (n_cross, slot_count), 1) < send_count[0, 0][:, None]
    )
    outgoing = jnp.where(live_slot[None], picked, 0.0)
    targets = recv_cells[0, 0].reshape(-1)
    weights = recv_coef[0, 0]
    arrived = lax.all_to_all(outgoing, "cross", split_axis=1, concat_axis=1, tiled=True)
    weighted = arrived * weights[None]
    empty = jnp.zeros((arrived.shape[0], flat_conc.shape[1]), jnp.float32)
    lateral = empty.at[:, targets].add(weighted.reshape(arrived.shape[0], -1))
    source = current + lateral.reshape(current.shape)
    return sweep(source, face_flux[0, 0], block_inverse[0, 0], upstream_block[0, 0])[None, None]


def solution(mesh):
    placed = (
        P("flow", "cross", None, None, None),
        P("flow", "cross", None, None, None),
        P("flow", "cross", None, None, None),
        P("flow", "cross", None),
        P("flow", "cross", None, None),
        P("flow", "cross", None),
        P("flow", "cross", None, None),
        P("flow", "cross", None, None),
    )
    return jax.shard_map(
        on_device,
        mesh=mesh,
        in_specs=placed,
        out_specs=P("flow", "cross", None, None, None),
        check_vma=False,
    )
```

```python
import jax
import jax.numpy as jnp
from jax import lax
from jax.experimental import pallas as pl
from jax.experimental.pallas import tpu as pltpu
from jax.sharding import PartitionSpec as P

MESH = pl.DeviceIdType.MESH
E, NB, B = 64, 8, 128
CELLS = NB * B
N_FLOW = 8
NX, NZ, NC = 4, 8, 2
GROUP = NX * NC
SUBS = 4
WIDE = 256


def split(value):
    high = value.astype(jnp.bfloat16)
    low = (value - high.astype(jnp.float32)).astype(jnp.bfloat16)
    return high, low


def dot(left, right):
    return jnp.dot(left, right, preferred_element_type=jnp.float32)


def dot3(left, right):
    left_high, left_low = left
    right_high, right_low = right
    return dot(left_high, right_high) + dot(left_low, right_high) + dot(left_high, right_low)


def one_hot(row, first, iota_ref):
    shifted = row - first
    inside = (shifted >= 0.0) & (shifted < float(WIDE))
    place = jnp.where(inside, shifted, -1.0).astype(jnp.bfloat16)
    hit = jnp.broadcast_to(place, (WIDE, WIDE)) == iota_ref[...]
    return jnp.where(hit, jnp.bfloat16(1), jnp.bfloat16(0))


def step_kernel(feeders, counts, conc_ref, flux_ref, inverse_ref, send_ref, cells_ref, coef_ref, out_ref,
                held, lhs, iota_ref, send_rows, zmeta, recv_rows, xmeta, xrow, weighted,
                to_partner, from_partner, comb, relay, final,
                resp_high, resp_low, src, local, incoming, outlet,
                right_send, right_recv, left_send, left_recv,
                zm_send, zm_recv, xm_send, xm_recv,
                pair_send, pair_recv, relay_send, relay_recv, final_send, final_recv,
                flow_send, flow_recv):
    flow = lax.axis_index("flow")
    cross = lax.axis_index("cross")
    x = cross // (NZ * NC)
    z = lax.rem(cross // NC, NZ)
    c = lax.rem(cross, NC)

    def peer(px, pz, pc):
        return {"cross": (px * NZ + pz) * NC + pc}

    def near(dx=0, dz=0, dc=0):
        return peer(lax.rem(x + dx + NX, NX), lax.rem(z + dz + NZ, NZ), lax.rem(c + dc, NC))

    flow_right = {"flow": lax.rem(flow + 1, N_FLOW)}
    flow_left = {"flow": lax.rem(flow + N_FLOW - 1, N_FLOW)}
    group = [(dx, dc) for dx in range(NX) for dc in range(NC)]

    barrier = pltpu.get_barrier_semaphore()
    greeted = [near(dz=k) for k in range(1, NZ)] + [near(dx=dx, dc=dc) for dx, dc in group[1:]]
    greeted += [flow_right, flow_left]
    for other in greeted:
        pl.semaphore_signal(barrier, inc=1, device_id=other, device_id_type=MESH)

    for b in range(NB):
        held[0, b] = conc_ref[:, b, :]
    lane = lax.broadcasted_iota(jnp.int32, (1, B), 1)
    for pz in range(NZ):
        for g in range(GROUP):
            peer_id = (g // NC) * NZ * NC + pz * NC + g % NC
            row = send_ref[pl.ds(peer_id, 1), :]
            live = jnp.where(lane < counts[peer_id], row, -1)
            send_rows[pz, pl.ds(g, 1), :] = live.astype(jnp.float32)
    for g in range(GROUP):
        rows = pl.ds((g // NC) * NZ * NC + g % NC, NZ, stride=NC)
        recv_rows[g, pl.ds(0, NZ), :] = cells_ref[rows, :].astype(jnp.float32)
        recv_rows[g, pl.ds(NZ, NZ), :] = coef_ref[rows, :]
    iota_ref[...] = lax.broadcasted_iota(jnp.int32, (WIDE, WIDE), 0).astype(jnp.float32).astype(jnp.bfloat16)

    def right_copy(r, i):
        part = pl.ds(2 * i, 2)
        return pltpu.make_async_remote_copy(
            src_ref=held.at[r, part], dst_ref=held.at[r + 1, part],
            send_sem=right_send.at[r, i], recv_sem=right_recv.at[r, i],
            device_id=near(dz=1), device_id_type=MESH)

    def left_copy(r, i):
        part = pl.ds(2 * i, 2)
        return pltpu.make_async_remote_copy(
            src_ref=held.at[(NZ - r) % NZ, part], dst_ref=held.at[NZ - r - 1, part],
            send_sem=left_send.at[r, i], recv_sem=left_recv.at[r, i],
            device_id=near(dz=-1), device_id_type=MESH)

    def zmeta_copy(k):
        return pltpu.make_async_remote_copy(
            src_ref=send_rows.at[lax.rem(z + k, NZ)], dst_ref=zmeta.at[k],
            send_sem=zm_send.at[k], recv_sem=zm_recv.at[k],
            device_id=near(dz=k), device_id_type=MESH)

    def xmeta_copy(dx, dc):
        to_x, to_c = lax.rem(x + NX - dx, NX), lax.rem(c + dc, NC)
        return pltpu.make_async_remote_copy(
            src_ref=recv_rows.at[to_x * NC + to_c], dst_ref=xmeta.at[dx * NC + dc],
            send_sem=xm_send.at[dx * NC + dc], recv_sem=xm_recv.at[dx * NC + dc],
            device_id=peer(to_x, z, to_c), device_id_type=MESH)

    def pair_copy(dx):
        return pltpu.make_async_remote_copy(
            src_ref=to_partner.at[dx], dst_ref=from_partner.at[dx],
            send_sem=pair_send.at[dx], recv_sem=pair_recv.at[dx],
            device_id=near(dc=1), device_id_type=MESH)

    def relay_copy(side):
        return pltpu.make_async_remote_copy(
            src_ref=comb.at[2, pl.ds(4 * side, 4)], dst_ref=relay.at[side],
            send_sem=relay_send.at[side], recv_sem=relay_recv.at[side],
            device_id=near(dx=1 - 2 * side), device_id_type=MESH)

    def final_copy(side, half):
        part = pl.ds(4 * half, 4)
        return pltpu.make_async_remote_copy(
            src_ref=comb.at[1 + 2 * side, part], dst_ref=final.at[side, part],
            send_sem=final_send.at[side, half], recv_sem=final_recv.at[side, half],
            device_id=near(dx=1 - 2 * side), device_id_type=MESH)

    flow_copy = pltpu.make_async_remote_copy(
        src_ref=outlet, dst_ref=incoming, send_sem=flow_send, recv_sem=flow_recv,
        device_id=flow_right, device_id_type=MESH)

    def response_start():
        resp_high[0] = jnp.zeros((CELLS + B, B), jnp.bfloat16)
        resp_low[0] = jnp.zeros((CELLS + B, B), jnp.bfloat16)
        own = split(inverse_ref[0])
        first = split(dot3(split(flux_ref[0]), own))
        resp_high[0, pl.ds(CELLS, B), :] = first[0]
        resp_low[0, pl.ds(CELLS, B), :] = first[1]
        resp_high[0, pl.ds(0, B), :] = own[0]
        resp_low[0, pl.ds(0, B), :] = own[1]

    def response_step(j):
        feeder = feeders[j]
        own = split(inverse_ref[j])
        step = split(dot3(split(flux_ref[j]), own))
        rows = split(dot3((resp_high[feeder], resp_low[feeder]), step))
        resp_high[j] = rows[0]
        resp_low[j] = rows[1]
        spot = pl.ds(pl.multiple_of(j * B, B), B)
        resp_high[j, spot, :] = own[0]
        resp_low[j, spot, :] = own[1]

    def load_lhs(r, which):
        for b in range(NB):
            high, low = split(held[r, b])
            lhs[which, pl.ds(0, E), pl.ds(b * B, B)] = high
            lhs[which, pl.ds(E, E), pl.ds(b * B, B)] = low

    def pick(r, which, p):
        at = lax.rem(x + p, NX) * NC
        row = jnp.concatenate(
            [zmeta[r, pl.ds(at + lax.rem(c + dc, NC), 1), :] for dc in range(NC)], axis=1)
        zs = NZ + lax.rem(z + NZ - r, NZ)
        coef = jnp.concatenate(
            [xmeta[p * NC + dc, pl.ds(zs, 1), :] for dc in range(NC)], axis=1)
        choice = jnp.concatenate([one_hot(row, float(WIDE * q), iota_ref) for q in range(SUBS)], axis=0)
        both = dot(lhs[which], choice)
        value = (both[:E] + both[E:]) * coef
        high, low = split(value)
        for dc in range(NC):
            weighted[p * NC + dc, pl.ds(0, E), pl.ds(r * B, B)] = high[:, dc * B:(dc + 1) * B]
            weighted[p * NC + dc, pl.ds(E, E), pl.ds(r * B, B)] = low[:, dc * B:(dc + 1) * B]

    def deposit(d, put):
        def chunk(q, carry):
            first = (q * WIDE).astype(jnp.float32)
            landing = jnp.concatenate(
                [one_hot(xrow[d, :, i * WIDE:(i + 1) * WIDE], first, iota_ref) for i in range(SUBS)], axis=1)
            both = lax.dot_general(weighted[d], landing, (((1,), (1,)), ((), ())),
                                   preferred_element_type=jnp.float32)
            value = both[:E] + both[E:]
            put[2 * q] = value[:, :B]
            put[2 * q + 1] = value[:, B:]
            return carry
        lax.fori_loop(0, SUBS, chunk, 0)

    pl.semaphore_wait(barrier, len(greeted))
    for k in range(1, NZ):
        zmeta_copy(k).start()
    for dx, dc in group[1:]:
        xmeta_copy(dx, dc).start()
    for i in range(SUBS):
        right_copy(0, i).start()
        left_copy(0, i).start()

    zmeta[0] = send_rows[z]
    xmeta[0] = recv_rows[x * NC + c]
    response_start()
    lax.fori_loop(1, 4, lambda j, carry: (response_step(j), carry)[1], 0)
    load_lhs(0, 0)
    for dx, dc in group[1:]:
        xmeta_copy(dx, dc).wait_recv()
    for d in range(GROUP):
        for r in range(NZ):
            xrow[d, :, pl.ds(r * B, B)] = xmeta[d, pl.ds(lax.rem(z + NZ - r, NZ), 1), :]

    for r in range(1, 4):
        if r > 1:
            zmeta_copy(r - 1).wait_recv()
            zmeta_copy(NZ - r + 1).wait_recv()
            load_lhs(r - 1, 0)
            load_lhs(NZ - r + 1, 1)

        def ring(i, carry, r=r):
            right_copy(r - 1, i).wait_recv()
            if r < 3:
                right_copy(r, i).start()
            else:
                @pl.when(i < 2)
                def _():
                    right_copy(r, i).start()
            left_copy(r - 1, i).wait_recv()
            if r < 3:
                left_copy(r, i).start()
            else:
                @pl.when(i >= 2)
                def _():
                    left_copy(r, i).start()
            if r == 1:
                response_step(4 + i)
                pick(0, 0, i)
            else:
                pick(r - 1, 0, i)
                pick(NZ - r + 1, 1, i)
            return carry

        lax.fori_loop(0, SUBS, ring, 0)

    zmeta_copy(3).wait_recv()
    zmeta_copy(5).wait_recv()
    zmeta_copy(4).wait_recv()
    load_lhs(3, 0)
    load_lhs(5, 1)

    def late(p, carry):
        pick(3, 0, p)
        pick(5, 1, p)
        return carry

    lax.fori_loop(0, SUBS, late, 0)
    for i in range(2):
        right_copy(3, i).wait_recv()
        left_copy(3, i + 2).wait_recv()
    load_lhs(4, 0)
    lax.fori_loop(0, SUBS, lambda p, carry: (pick(4, 0, p), carry)[1], 0)

    def combine(dx):
        pair_copy(dx).wait_recv()
        comb[dx] = comb[dx] + from_partner[dx]

    deposit(2 * NC + 1, to_partner.at[2])
    pair_copy(2).start()
    deposit(2 * NC, comb.at[2])
    deposit(1 * NC + 1, to_partner.at[1])
    pair_copy(1).start()
    combine(2)
    relay_copy(0).start()
    relay_copy(1).start()
    deposit(1 * NC, comb.at[1])
    deposit(3 * NC + 1, to_partner.at[3])
    pair_copy(3).start()
    combine(1)
    final_copy(0, 1).start()
    deposit(3 * NC, comb.at[3])
    deposit(1, to_partner.at[0])
    pair_copy(0).start()
    combine(3)
    final_copy(1, 0).start()
    relay_copy(0).wait_recv()
    comb[1, pl.ds(0, 4)] = comb[1, pl.ds(0, 4)] + relay[0]
    final_copy(0, 0).start()
    relay_copy(1).wait_recv()
    comb[3, pl.ds(4, 4)] = comb[3, pl.ds(4, 4)] + relay[1]
    final_copy(1, 1).start()
    deposit(0, comb.at[0])
    combine(0)
    comb[0] = comb[0] + held[0]
    for side, half in ((0, 1), (1, 0), (0, 0), (1, 1)):
        final_copy(side, half).wait_recv()
    for b in range(NB):
        high, low = split(comb[0, b] + final[0, b] + final[1, b])
        src[pl.ds(0, E), pl.ds(b * B, B)] = high
        src[pl.ds(E, E), pl.ds(b * B, B)] = low

    def solve(j):
        both = dot(src[...], resp_high[j, pl.ds(0, CELLS), :])
        return both[:E] + both[E:] + dot(src[pl.ds(0, E), :], resp_low[j, pl.ds(0, CELLS), :])

    def entering(j, parts):
        return dot3(parts, (resp_high[j, pl.ds(CELLS, B), :], resp_low[j, pl.ds(CELLS, B), :]))

    last = solve(NB - 1)

    @pl.when(flow == 0)
    def _():
        outlet[...] = last
        flow_copy.start()
        incoming[...] = jnp.zeros_like(incoming)

    for j in range(NB - 1):
        local[j] = solve(j)

    @pl.when(flow > 0)
    def _():
        flow_copy.wait_recv()
        outlet[...] = last + entering(NB - 1, split(incoming[...]))

        @pl.when(flow < N_FLOW - 1)
        def _():
            flow_copy.start()

    out_ref[:, NB - 1, :] = outlet[...]
    parts = split(incoming[...])
    for j in range(NB - 1):
        out_ref[:, j, :] = local[j] + entering(j, parts)

    for k in range(1, NZ):
        zmeta_copy(k).wait_send()
    for dx, dc in group[1:]:
        xmeta_copy(dx, dc).wait_send()
    for r in range(3):
        for i in range(SUBS):
            right_copy(r, i).wait_send()
            left_copy(r, i).wait_send()
    for i in range(2):
        right_copy(3, i).wait_send()
        left_copy(3, i + 2).wait_send()
    for dx in range(NX):
        pair_copy(dx).wait_send()
    for side in range(2):
        relay_copy(side).wait_send()
        for half in range(2):
            final_copy(side, half).wait_send()

    @pl.when(flow < N_FLOW - 1)
    def _():
        flow_copy.wait_send()


def step(feeders, counts, conc, couplings, inverses, send_cells, recv_cells, recv_coef):
    vmem = pl.BlockSpec(memory_space=pltpu.VMEM)
    smem = pl.BlockSpec(memory_space=pltpu.SMEM)
    f32, bf16 = jnp.float32, jnp.bfloat16
    dma = pltpu.SemaphoreType.DMA
    return pl.pallas_call(
        step_kernel,
        out_shape=jax.ShapeDtypeStruct((E, NB, B), f32),
        in_specs=[smem, smem] + [vmem] * 6,
        out_specs=vmem,
        scratch_shapes=[
            pltpu.VMEM((NZ, NB, E, B), f32),
            pltpu.VMEM((2, 2 * E, CELLS), bf16),
            pltpu.VMEM((WIDE, WIDE), bf16),
            pltpu.VMEM((NZ, GROUP, B), f32),
            pltpu.VMEM((NZ, GROUP, B), f32),
            pltpu.VMEM((GROUP, 2 * NZ, B), f32),
            pltpu.VMEM((GROUP, 2 * NZ, B), f32),
            pltpu.VMEM((GROUP, 1, CELLS), f32),
            pltpu.VMEM((GROUP, 2 * E, CELLS), bf16),
            pltpu.VMEM((NX, NB, E, B), f32),
            pltpu.VMEM((NX, NB, E, B), f32),
            pltpu.VMEM((NX, NB, E, B), f32),
            pltpu.VMEM((2, 4, E, B), f32),
            pltpu.VMEM((2, NB, E, B), f32),
            pltpu.VMEM((NB, CELLS + B, B), bf16),
            pltpu.VMEM((NB, CELLS + B, B), bf16),
            pltpu.VMEM((2 * E, CELLS), bf16),
            pltpu.VMEM((NB, E, B), f32),
            pltpu.VMEM((E, B), f32),
            pltpu.VMEM((E, B), f32),
            dma((4, SUBS)), dma((4, SUBS)), dma((4, SUBS)), dma((4, SUBS)),
            dma((NZ,)), dma((NZ,)), dma((GROUP,)), dma((GROUP,)),
            dma((NX,)), dma((NX,)), dma((2,)), dma((2,)), dma((2, 2)), dma((2, 2)),
            dma, dma,
        ],
        compiler_params=pltpu.CompilerParams(collective_id=0, has_side_effects=True),
        name="transport_step",
    )(feeders, counts, conc, couplings, inverses, send_cells, recv_cells, recv_coef)


def on_device(conc_old, face_flux, block_inverse, upstream_block, send_cells, send_count, recv_cells, recv_coef):
    return step(
        upstream_block[0, 0], send_count[0, 0], conc_old[0, 0], face_flux[0, 0], block_inverse[0, 0],
        send_cells[0, 0], recv_cells[0, 0], recv_coef[0, 0])[None, None]


def solution(mesh):
    placed = (
        P("flow", "cross", None, None, None),
        P("flow", "cross", None, None, None),
        P("flow", "cross", None, None, None),
        P("flow", "cross", None),
        P("flow", "cross", None, None),
        P("flow", "cross", None),
        P("flow", "cross", None, None),
        P("flow", "cross", None, None),
    )
    return jax.shard_map(
        on_device,
        mesh=mesh,
        in_specs=placed,
        out_specs=P("flow", "cross", None, None, None),
        check_vma=False,
    )
```

```python
import jax
import jax.numpy as jnp
from jax import lax
from jax.experimental import pallas as pl
from jax.experimental.pallas import tpu as pltpu
from jax.sharding import PartitionSpec as P

MESH = pl.DeviceIdType.MESH
E, NB, B = 64, 8, 128
CELLS = NB * B
N_FLOW = 8
NX, NZ, NC = 4, 8, 2
GROUP = NX * NC
SUBS = 4
WIDE = 256
ORDER = ((0, 1), (7, 2), (6, 3), (5, 4))
WHERE = {r: (t, half) for t, pair in enumerate(ORDER) for half, r in enumerate(pair)}


def split(value):
    high = value.astype(jnp.bfloat16)
    low = (value - high.astype(jnp.float32)).astype(jnp.bfloat16)
    return high, low


def dot(left, right):
    return jnp.dot(left, right, preferred_element_type=jnp.float32)


def dot3(left, right):
    left_high, left_low = left
    right_high, right_low = right
    return dot(left_high, right_high) + dot(left_low, right_high) + dot(left_high, right_low)


def one_hot(row, first, iota_ref):
    shifted = row - first
    inside = (shifted >= 0.0) & (shifted < float(WIDE))
    place = jnp.where(inside, shifted, -1.0).astype(jnp.bfloat16)
    hit = jnp.broadcast_to(place, (WIDE, WIDE)) == iota_ref[...]
    return jnp.where(hit, jnp.bfloat16(1), jnp.bfloat16(0))


def scaled_rows(matrix):
    top = jnp.maximum(jnp.max(matrix, axis=1, keepdims=True), 1e-30)
    column = jnp.broadcast_to(top, (B, B))
    return matrix / column, jnp.transpose(column)[0:1, :]


def step_kernel(feeders_in, counts_in, conc_in, flux_in, inverse_in, send_in, cells_in, coef_in,
                settled_ref, entered_ref,
                feeders, counts, conc_ref, flux_ref, inverse_ref, send_ref, cells_ref, coef_ref,
                held, lhs, iota_ref, send_rows, zmeta, recv_rows, xmeta, xrow, weighted,
                to_partner, from_partner, comb, relay, final,
                resp_high, resp_low, src, outlet, passing, above, passages,
                chain_high, chain_low, chain_scale, arriving,
                load_sem,
                right_send, right_recv, left_send, left_recv,
                zm_send, zm_recv, xm_send, xm_recv,
                pair_send, pair_recv, relay_send, relay_recv, final_send, final_recv,
                above_send, above_recv, pass_send, pass_recv):
    flow = lax.axis_index("flow")
    cross = lax.axis_index("cross")
    x = cross // (NZ * NC)
    z = lax.rem(cross // NC, NZ)
    c = lax.rem(cross, NC)

    def peer(px, pz, pc):
        return {"cross": (px * NZ + pz) * NC + pc}

    def near(dx=0, dz=0, dc=0):
        return peer(lax.rem(x + dx + NX, NX), lax.rem(z + dz + NZ, NZ), lax.rem(c + dc, NC))

    group = [(dx, dc) for dx in range(NX) for dc in range(NC)]

    barrier = pltpu.get_barrier_semaphore()
    greeted = [near(dz=k) for k in range(1, NZ)] + [near(dx=dx, dc=dc) for dx, dc in group[1:]]
    greeted += [{"flow": lax.rem(flow + k, N_FLOW)} for k in range(1, N_FLOW)]
    for other in greeted:
        pl.semaphore_signal(barrier, inc=1, device_id=other, device_id_type=MESH)

    loads = [pltpu.make_async_copy(a, b, load_sem.at[i]) for i, (a, b) in enumerate((
        (conc_in, conc_ref), (counts_in, counts), (send_in, send_ref), (cells_in, cells_ref),
        (coef_in, coef_ref), (feeders_in, feeders), (flux_in, flux_ref), (inverse_in, inverse_ref)))]
    for load in loads:
        load.start()
    iota_ref[...] = lax.broadcasted_iota(jnp.int32, (WIDE, WIDE), 0).astype(jnp.float32).astype(jnp.bfloat16)
    for k in range(1, N_FLOW):
        @pl.when(flow < k)
        def _(k=k):
            above[k - 1] = jnp.zeros((E, B), jnp.float32)
    for k in range(1, N_FLOW - 1):
        @pl.when(flow <= k)
        def _(k=k):
            passages[k - 1] = jnp.zeros((B, B), jnp.float32)
    loads[0].wait()
    for b in range(NB):
        held[0, b] = conc_ref[:, b, :]
    for load in loads[1:5]:
        load.wait()
    lane = lax.broadcasted_iota(jnp.int32, (1, B), 1)
    for pz in range(NZ):
        for g in range(GROUP):
            peer_id = (g // NC) * NZ * NC + pz * NC + g % NC
            row = send_ref[pl.ds(peer_id, 1), :]
            live = jnp.where(lane < counts[peer_id], row, -1)
            send_rows[pz, pl.ds(g, 1), :] = live.astype(jnp.float32)
    for g in range(GROUP):
        rows = pl.ds((g // NC) * NZ * NC + g % NC, NZ, stride=NC)
        recv_rows[g, pl.ds(0, NZ), :] = cells_ref[rows, :].astype(jnp.float32)
        recv_rows[g, pl.ds(NZ, NZ), :] = coef_ref[rows, :]

    def right_copy(r, i):
        part = pl.ds(2 * i, 2)
        return pltpu.make_async_remote_copy(
            src_ref=held.at[r, part], dst_ref=held.at[r + 1, part],
            send_sem=right_send.at[r, i], recv_sem=right_recv.at[r, i],
            device_id=near(dz=1), device_id_type=MESH)

    def left_copy(r, i):
        part = pl.ds(2 * i, 2)
        return pltpu.make_async_remote_copy(
            src_ref=held.at[(NZ - r) % NZ, part], dst_ref=held.at[NZ - r - 1, part],
            send_sem=left_send.at[r, i], recv_sem=left_recv.at[r, i],
            device_id=near(dz=-1), device_id_type=MESH)

    def zmeta_copy(k):
        return pltpu.make_async_remote_copy(
            src_ref=send_rows.at[lax.rem(z + k, NZ)], dst_ref=zmeta.at[k],
            send_sem=zm_send.at[k], recv_sem=zm_recv.at[k],
            device_id=near(dz=k), device_id_type=MESH)

    def xmeta_copy(dx, dc):
        to_x, to_c = lax.rem(x + NX - dx, NX), lax.rem(c + dc, NC)
        return pltpu.make_async_remote_copy(
            src_ref=recv_rows.at[to_x * NC + to_c], dst_ref=xmeta.at[dx * NC + dc],
            send_sem=xm_send.at[dx * NC + dc], recv_sem=xm_recv.at[dx * NC + dc],
            device_id=peer(to_x, z, to_c), device_id_type=MESH)

    def pair_copy(dx, q):
        part = pl.ds(2 * q, 2)
        return pltpu.make_async_remote_copy(
            src_ref=to_partner.at[dx, part], dst_ref=from_partner.at[dx, part],
            send_sem=pair_send.at[dx, q], recv_sem=pair_recv.at[dx, q],
            device_id=near(dc=1), device_id_type=MESH)

    def relay_copy(q):
        return pltpu.make_async_remote_copy(
            src_ref=comb.at[2, pl.ds(2 * q, 2)], dst_ref=relay.at[q],
            send_sem=relay_send.at[q], recv_sem=relay_recv.at[q],
            device_id=near(dx=1 if q < 2 else -1), device_id_type=MESH)

    def final_copy(side, q):
        part = pl.ds(2 * q, 2)
        return pltpu.make_async_remote_copy(
            src_ref=comb.at[1 + 2 * side, part], dst_ref=final.at[side, part],
            send_sem=final_send.at[side, q], recv_sem=final_recv.at[side, q],
            device_id=near(dx=1 - 2 * side), device_id_type=MESH)

    def above_copy(k):
        return pltpu.make_async_remote_copy(
            src_ref=outlet, dst_ref=above.at[k - 1],
            send_sem=above_send.at[k - 1], recv_sem=above_recv.at[k - 1],
            device_id={"flow": lax.rem(flow + k, N_FLOW)}, device_id_type=MESH)

    def pass_copy(k):
        return pltpu.make_async_remote_copy(
            src_ref=passing, dst_ref=passages.at[k - 1],
            send_sem=pass_send.at[k - 1], recv_sem=pass_recv.at[k - 1],
            device_id={"flow": lax.rem(flow + k, N_FLOW)}, device_id_type=MESH)

    def response_start():
        resp_high[0] = jnp.zeros((CELLS + B, B), jnp.bfloat16)
        resp_low[0] = jnp.zeros((CELLS + B, B), jnp.bfloat16)
        own = split(inverse_ref[0])
        first = split(dot3(split(flux_ref[0]), own))
        resp_high[0, pl.ds(CELLS, B), :] = first[0]
        resp_low[0, pl.ds(CELLS, B), :] = first[1]
        resp_high[0, pl.ds(0, B), :] = own[0]
        resp_low[0, pl.ds(0, B), :] = own[1]

    def response_step(j):
        feeder = feeders[j]
        own = split(inverse_ref[j])
        step = split(dot3(split(flux_ref[j]), own))
        rows = split(dot3((resp_high[feeder], resp_low[feeder]), step))
        resp_high[j] = rows[0]
        resp_low[j] = rows[1]
        spot = pl.ds(pl.multiple_of(j * B, B), B)
        resp_high[j, spot, :] = own[0]
        resp_low[j, spot, :] = own[1]

    def load_lhs(r, which):
        for b in range(NB):
            high, low = split(held[r, b])
            lhs[which, pl.ds(0, E), pl.ds(b * B, B)] = high
            lhs[which, pl.ds(E, E), pl.ds(b * B, B)] = low

    def pick(r, which, p):
        at = lax.rem(x + p, NX) * NC
        row = jnp.concatenate(
            [zmeta[r, pl.ds(at + lax.rem(c + dc, NC), 1), :] for dc in range(NC)], axis=1)
        zs = NZ + lax.rem(z + NZ - r, NZ)
        coef = jnp.concatenate(
            [xmeta[p * NC + dc, pl.ds(zs, 1), :] for dc in range(NC)], axis=1)
        choice = jnp.concatenate([one_hot(row, float(WIDE * q), iota_ref) for q in range(SUBS)], axis=0)
        both = dot(lhs[which], choice)
        value = (both[:E] + both[E:]) * coef
        high, low = split(value)
        t, half = WHERE[r]
        lanes = pl.ds(half * B, B)
        for dc in range(NC):
            weighted[p * NC + dc, t, pl.ds(0, E), lanes] = high[:, dc * B:(dc + 1) * B]
            weighted[p * NC + dc, t, pl.ds(E, E), lanes] = low[:, dc * B:(dc + 1) * B]

    def deposit(p, dc, t, q):
        put = to_partner if dc else comb
        landing = one_hot(xrow[p * NC + dc, t], float(WIDE * q), iota_ref)
        both = lax.dot_general(weighted[p * NC + dc, t], landing, (((1,), (1,)), ((), ())),
                               preferred_element_type=jnp.float32)
        value = both[:E] + both[E:]
        for i in range(2):
            piece = value[:, i * B:(i + 1) * B]
            put[p, 2 * q + i] = piece if t == 0 else put[p, 2 * q + i] + piece

    def deposit_all(p, t):
        for q in range(SUBS):
            for dc in range(NC):
                deposit(p, dc, t, q)

    pl.semaphore_wait(barrier, len(greeted))
    for k in range(1, NZ):
        zmeta_copy(k).start()
    for dx, dc in group[1:]:
        xmeta_copy(dx, dc).start()
    for i in range(SUBS):
        right_copy(0, i).start()
        left_copy(0, i).start()

    for load in loads[5:]:
        load.wait()
    zmeta[0] = send_rows[z]
    xmeta[0] = recv_rows[x * NC + c]
    response_start()
    lax.fori_loop(1, 4, lambda j, carry: (response_step(j), carry)[1], 0)
    load_lhs(0, 0)
    for dx, dc in group[1:]:
        xmeta_copy(dx, dc).wait_recv()
    for d in range(GROUP):
        for r in range(NZ):
            t, half = WHERE[r]
            xrow[d, t, :, pl.ds(half * B, B)] = xmeta[d, pl.ds(lax.rem(z + NZ - r, NZ), 1), :]

    for r in range(1, 4):
        if r > 1:
            zmeta_copy(r - 1).wait_recv()
            zmeta_copy(NZ - r + 1).wait_recv()
            load_lhs(r - 1, 0)
            load_lhs(NZ - r + 1, 1)

        def ring(i, carry, r=r):
            right_copy(r - 1, i).wait_recv()
            if r < 3:
                right_copy(r, i).start()
            else:
                @pl.when(i < 2)
                def _():
                    right_copy(r, i).start()
            left_copy(r - 1, i).wait_recv()
            if r < 3:
                left_copy(r, i).start()
            else:
                @pl.when(i >= 2)
                def _():
                    left_copy(r, i).start()
            if r == 1:
                response_step(4 + i)
                pick(0, 0, i)
            else:
                pick(r - 1, 0, i)
                pick(NZ - r + 1, 1, i)
                deposit_all(i, r - 2)
            return carry

        lax.fori_loop(0, SUBS, ring, 0)
        if r == 1:
            passing[...] = (resp_high[NB - 1, pl.ds(CELLS, B), :].astype(jnp.float32)
                            + resp_low[NB - 1, pl.ds(CELLS, B), :].astype(jnp.float32))
            for k in range(1, N_FLOW - 1):
                @pl.when((flow >= 1) & (flow + k < N_FLOW))
                def _(k=k):
                    pass_copy(k).start()

    zmeta_copy(3).wait_recv()
    zmeta_copy(5).wait_recv()
    zmeta_copy(4).wait_recv()
    load_lhs(3, 0)
    load_lhs(5, 1)

    def late(p, carry):
        pick(3, 0, p)
        pick(5, 1, p)
        deposit_all(p, 2)
        return carry

    lax.fori_loop(0, SUBS, late, 0)
    for i in range(2):
        right_copy(3, i).wait_recv()
        left_copy(3, i + 2).wait_recv()
    load_lhs(4, 0)

    def finish(p, q):
        deposit(p, 1, 3, q)
        pair_copy(p, q).start()
        deposit(p, 0, 3, q)

    def combine(p, q):
        pair_copy(p, q).wait_recv()
        part = pl.ds(2 * q, 2)
        comb[p, part] = comb[p, part] + from_partner[p, part]

    pick(4, 0, 2)
    for q in range(SUBS):
        finish(2, q)
    pick(4, 0, 1)
    pick(4, 0, 3)
    for q in (0, 2, 1, 3):
        combine(2, q)
        relay_copy(q).start()
    early = ((0, 2), (1, 0), (0, 3), (1, 1))
    later = ((0, 0), (1, 2), (0, 1), (1, 3))
    for side, q in early:
        finish(1 + 2 * side, q)
    for side, q in early:
        combine(1 + 2 * side, q)
        final_copy(side, q).start()
    for side, q in later:
        finish(1 + 2 * side, q)
    for side, q in later:
        combine(1 + 2 * side, q)
    pick(4, 0, 0)
    for q in range(SUBS):
        finish(0, q)
    for side, q in later:
        relay_copy(q).wait_recv()
        part = pl.ds(2 * q, 2)
        comb[1 + 2 * side, part] = comb[1 + 2 * side, part] + relay[q]
        final_copy(side, q).start()
    for q in range(SUBS):
        combine(0, q)
    comb[0] = comb[0] + held[0]

    for k in range(1, N_FLOW - 1):
        @pl.when(flow > k)
        def _(k=k):
            pass_copy(k).wait_recv()
    link = [split(passages[k]) for k in range(N_FLOW - 2)]
    two, four, six = (dot3(link[2 * i + 1], link[2 * i]) for i in range(3))
    two_parts, four_parts = split(two), split(four)
    whole_five, scale_five = scaled_rows(passages[4])
    whole_six, scale_six = scaled_rows(six)
    upper = dot3(split(jnp.concatenate([whole_five, whole_six], axis=0)), four_parts)
    whole_three, scale_three = scaled_rows(passages[2])
    whole_four, scale_four = scaled_rows(four)
    upper_five, more_five = scaled_rows(upper[:B])
    upper_six, more_six = scaled_rows(upper[B:])
    longer = dot3(split(jnp.concatenate([whole_three, whole_four, upper_five, upper_six], axis=0)), two_parts)
    for k, matrix in enumerate((link[0], two_parts)):
        chain_high[pl.ds(k * B, B), :] = matrix[0]
        chain_low[pl.ds(k * B, B), :] = matrix[1]
    longer_parts = split(longer)
    chain_high[pl.ds(2 * B, 4 * B), :] = longer_parts[0]
    chain_low[pl.ds(2 * B, 4 * B), :] = longer_parts[1]
    ones = jnp.ones((1, B), jnp.float32)
    for k, (first, second) in enumerate((
            (ones, ones), (ones, ones), (scale_three, ones), (scale_four, ones),
            (scale_five, more_five), (scale_six, more_six))):
        chain_scale[k, pl.ds(0, 1), :] = first
        chain_scale[k, pl.ds(1, 1), :] = second

    for side, q in early:
        final_copy(side, q).wait_recv()
        part = pl.ds(2 * q, 2)
        comb[0, part] = comb[0, part] + final[side, part]
    for side, q in later:
        final_copy(side, q).wait_recv()
        for b in (2 * q, 2 * q + 1):
            high, low = split(comb[0, b] + final[side, b])
            src[pl.ds(0, E), pl.ds(b * B, B)] = high
            src[pl.ds(E, E), pl.ds(b * B, B)] = low

    def solve(j):
        both = dot(src[...], resp_high[j, pl.ds(0, CELLS), :])
        return both[:E] + both[E:] + dot(src[pl.ds(0, E), :], resp_low[j, pl.ds(0, CELLS), :])

    outlet[...] = solve(NB - 1)
    for k in (4, 3, 5, 2, 6, 1, 7):
        @pl.when(flow + k < N_FLOW)
        def _(k=k):
            above_copy(k).start()
    settled_ref[:, NB - 1, :] = outlet[...]
    for j in range(NB - 1):
        settled_ref[:, j, :] = solve(j)

    for k in (7, 6, 5, 4, 3, 2, 1):
        @pl.when(flow >= k)
        def _(k=k):
            above_copy(k).wait_recv()
        if k > 1:
            high, low = split(above[k - 1] * chain_scale[k - 2, pl.ds(0, 1), :] * chain_scale[k - 2, pl.ds(1, 1), :])
            arriving[pl.ds(0, E), pl.ds((k - 2) * B, B)] = high
            arriving[pl.ds(E, E), pl.ds((k - 2) * B, B)] = low
    both = dot(arriving[...], chain_high[...])
    inflow = above[0] + both[:E] + both[E:] + dot(arriving[pl.ds(0, E), :], chain_low[...])
    parts = split(inflow)
    for j in range(NB):
        entered_ref[:, j, :] = dot3(parts, (resp_high[j, pl.ds(CELLS, B), :], resp_low[j, pl.ds(CELLS, B), :]))

    for k in range(1, NZ):
        zmeta_copy(k).wait_send()
    for dx, dc in group[1:]:
        xmeta_copy(dx, dc).wait_send()
    for r in range(3):
        for i in range(SUBS):
            right_copy(r, i).wait_send()
            left_copy(r, i).wait_send()
    for i in range(2):
        right_copy(3, i).wait_send()
        left_copy(3, i + 2).wait_send()
    for q in range(SUBS):
        for dx in range(NX):
            pair_copy(dx, q).wait_send()
        relay_copy(q).wait_send()
        for side in range(2):
            final_copy(side, q).wait_send()
    for k in range(1, N_FLOW):
        @pl.when(flow + k < N_FLOW)
        def _(k=k):
            above_copy(k).wait_send()
    for k in range(1, N_FLOW - 1):
        @pl.when((flow >= 1) & (flow + k < N_FLOW))
        def _(k=k):
            pass_copy(k).wait_send()


def step(feeders, counts, conc, couplings, inverses, send_cells, recv_cells, recv_coef):
    vmem = pl.BlockSpec(memory_space=pltpu.VMEM)
    f32, bf16, i32 = jnp.float32, jnp.bfloat16, jnp.int32
    dma = pltpu.SemaphoreType.DMA
    settled, entered = pl.pallas_call(
        step_kernel,
        out_shape=[jax.ShapeDtypeStruct((E, NB, B), f32)] * 2,
        in_specs=[pl.BlockSpec(memory_space=pl.ANY)] * 8,
        out_specs=[vmem, vmem],
        scratch_shapes=[
            pltpu.SMEM((NB,), i32),
            pltpu.SMEM((NZ * GROUP,), i32),
            pltpu.VMEM((E, NB, B), f32),
            pltpu.VMEM((NB, B, B), f32),
            pltpu.VMEM((NB, B, B), f32),
            pltpu.VMEM((NZ * GROUP, B), i32),
            pltpu.VMEM((NZ * GROUP, B), i32),
            pltpu.VMEM((NZ * GROUP, B), f32),
            pltpu.VMEM((NZ, NB, E, B), f32),
            pltpu.VMEM((2, 2 * E, CELLS), bf16),
            pltpu.VMEM((WIDE, WIDE), bf16),
            pltpu.VMEM((NZ, GROUP, B), f32),
            pltpu.VMEM((NZ, GROUP, B), f32),
            pltpu.VMEM((GROUP, 2 * NZ, B), f32),
            pltpu.VMEM((GROUP, 2 * NZ, B), f32),
            pltpu.VMEM((GROUP, SUBS, 1, WIDE), f32),
            pltpu.VMEM((GROUP, SUBS, 2 * E, WIDE), bf16),
            pltpu.VMEM((NX, NB, E, B), f32),
            pltpu.VMEM((NX, NB, E, B), f32),
            pltpu.VMEM((NX, NB, E, B), f32),
            pltpu.VMEM((SUBS, 2, E, B), f32),
            pltpu.VMEM((2, NB, E, B), f32),
            pltpu.VMEM((NB, CELLS + B, B), bf16),
            pltpu.VMEM((NB, CELLS + B, B), bf16),
            pltpu.VMEM((2 * E, CELLS), bf16),
            pltpu.VMEM((E, B), f32),
            pltpu.VMEM((B, B), f32),
            pltpu.VMEM((N_FLOW - 1, E, B), f32),
            pltpu.VMEM((N_FLOW - 2, B, B), f32),
            pltpu.VMEM(((N_FLOW - 2) * B, B), bf16),
            pltpu.VMEM(((N_FLOW - 2) * B, B), bf16),
            pltpu.VMEM((N_FLOW - 2, 8, B), f32),
            pltpu.VMEM((2 * E, (N_FLOW - 2) * B), bf16),
            dma((8,)),
            dma((4, SUBS)), dma((4, SUBS)), dma((4, SUBS)), dma((4, SUBS)),
            dma((NZ,)), dma((NZ,)), dma((GROUP,)), dma((GROUP,)),
            dma((NX, SUBS)), dma((NX, SUBS)), dma((SUBS,)), dma((SUBS,)), dma((2, SUBS)), dma((2, SUBS)),
            dma((N_FLOW - 1,)), dma((N_FLOW - 1,)), dma((N_FLOW - 2,)), dma((N_FLOW - 2,)),
        ],
        compiler_params=pltpu.CompilerParams(collective_id=0, has_side_effects=True),
        name="transport_step",
    )(feeders, counts, conc, couplings, inverses, send_cells, recv_cells, recv_coef)
    return settled + entered


def on_device(conc_old, face_flux, block_inverse, upstream_block, send_cells, send_count, recv_cells, recv_coef):
    return step(
        upstream_block[0, 0], send_count[0, 0], conc_old[0, 0], face_flux[0, 0], block_inverse[0, 0],
        send_cells[0, 0], recv_cells[0, 0], recv_coef[0, 0])[None, None]


def solution(mesh):
    placed = (
        P("flow", "cross", None, None, None),
        P("flow", "cross", None, None, None),
        P("flow", "cross", None, None, None),
        P("flow", "cross", None),
        P("flow", "cross", None, None),
        P("flow", "cross", None),
        P("flow", "cross", None, None),
        P("flow", "cross", None, None),
    )
    return jax.shard_map(
        on_device,
        mesh=mesh,
        in_specs=placed,
        out_specs=P("flow", "cross", None, None, None),
        check_vma=False,
    )
```

```python
import jax
import jax.numpy as jnp
from jax import lax
from jax.experimental import pallas as pl
from jax.experimental.pallas import tpu as pltpu
from jax.sharding import PartitionSpec as P

MESH = pl.DeviceIdType.MESH
E, NB, B = 64, 8, 128
CELLS = NB * B
N_FLOW = 8
NX, NZ, NC = 4, 8, 2
GROUP = NX * NC
SUBS = 4
WIDE = 256
ORDER = ((0, 1), (7, 2), (6, 3), (5, 4))
WHERE = {r: (t, half) for t, pair in enumerate(ORDER) for half, r in enumerate(pair)}


def split(value):
    high = value.astype(jnp.bfloat16)
    low = (value - high.astype(jnp.float32)).astype(jnp.bfloat16)
    return high, low


def dot(left, right):
    return jnp.dot(left, right, preferred_element_type=jnp.float32)


def beside(value):
    return jnp.concatenate(split(value), axis=1)


def product(left, right):
    high, low = split(right)
    whole = jnp.concatenate([jnp.concatenate([high, low], axis=1),
                             jnp.concatenate([high, jnp.zeros_like(low)], axis=1)], axis=0)
    both = dot(left, whole)
    return both[:, :B] + both[:, B:]


def corners(both):
    return both[:E, :B] + both[E:, :B] + both[:E, B:]


def one_hot(row, first, iota_ref):
    shifted = row - first
    inside = (shifted >= 0.0) & (shifted < float(WIDE))
    place = jnp.where(inside, shifted, -1.0).astype(jnp.bfloat16)
    hit = jnp.broadcast_to(place, (WIDE, WIDE)) == iota_ref[...]
    return jnp.where(hit, jnp.bfloat16(1), jnp.bfloat16(0))


def scaled_rows(matrix):
    top = jnp.maximum(jnp.max(matrix, axis=1, keepdims=True), 1e-30)
    column = jnp.broadcast_to(top, (B, B))
    return matrix / column, jnp.transpose(column)[0:1, :]


def step_kernel(feeders_in, counts_in, conc_in, flux_in, inverse_in, send_in, cells_in, coef_in,
                settled_ref, entered_ref,
                feeders, counts, conc_ref, flux_ref, inverse_ref, send_ref, cells_ref, coef_ref,
                held, lhs, iota_ref, send_rows, lists, recv_rows, xmeta, xrow, weighted,
                to_partner, from_partner, comb, relay, final,
                resp, src, outlet, passing, above, passages,
                chain, chain_scale, arriving,
                load_sem,
                right_send, right_recv, left_send, left_recv,
                list_send, list_recv, xm_send, xm_recv,
                pair_send, pair_recv, relay_send, relay_recv, final_send, final_recv,
                above_send, above_recv, pass_send, pass_recv, rounds):
    flow = lax.axis_index("flow")
    cross = lax.axis_index("cross")
    x = cross // (NZ * NC)
    z = lax.rem(cross // NC, NZ)
    c = lax.rem(cross, NC)

    def peer(px, pz, pc):
        return {"cross": (px * NZ + pz) * NC + pc}

    def near(dx=0, dz=0, dc=0):
        return peer(lax.rem(x + dx + NX, NX), lax.rem(z + dz + NZ, NZ), lax.rem(c + dc, NC))

    group = [(dx, dc) for dx in range(NX) for dc in range(NC)]

    barrier = pltpu.get_barrier_semaphore()
    flow_near = [{"flow": lax.rem(flow + k, N_FLOW)} for k in (1, N_FLOW - 1)]
    greeted = [near(dz=1), near(dz=-1)] + [near(dx=dx, dc=dc) for dx, dc in group[1:]] + flow_near
    for other in greeted:
        pl.semaphore_signal(barrier, inc=1, device_id=other, device_id_type=MESH)

    loads = [pltpu.make_async_copy(a, b, load_sem.at[i]) for i, (a, b) in enumerate((
        (conc_in, conc_ref), (counts_in, counts), (send_in, send_ref), (cells_in, cells_ref),
        (coef_in, coef_ref), (feeders_in, feeders), (flux_in, flux_ref), (inverse_in, inverse_ref)))]
    for load in loads:
        load.start()
    iota_ref[...] = lax.broadcasted_iota(jnp.int32, (WIDE, WIDE), 0).astype(jnp.float32).astype(jnp.bfloat16)
    for k in range(1, N_FLOW):
        @pl.when(flow < k)
        def _(k=k):
            above[k - 1] = jnp.zeros((E, B), jnp.float32)
    for k in range(1, N_FLOW - 1):
        @pl.when(flow <= k)
        def _(k=k):
            passages[k - 1] = jnp.zeros((B, B), jnp.float32)
    loads[0].wait()
    for b in range(NB):
        held[0, b] = conc_ref[:, b, :]
    for load in loads[1:5]:
        load.wait()
    lane = lax.broadcasted_iota(jnp.int32, (1, B), 1)
    for pz in range(NZ):
        for g in range(GROUP):
            peer_id = (g // NC) * NZ * NC + pz * NC + g % NC
            row = send_ref[pl.ds(peer_id, 1), :]
            live = jnp.where(lane < counts[peer_id], row, -1)
            send_rows[pz, pl.ds(g, 1), :] = live.astype(jnp.float32)
    for k in range(SUBS):
        lists[0, 0, k] = send_rows[lax.rem(z + k + 1, NZ)]
    for k in range(SUBS - 1):
        lists[1, 0, k] = send_rows[lax.rem(z + NZ - k - 1, NZ)]
    for g in range(GROUP):
        rows = pl.ds((g // NC) * NZ * NC + g % NC, NZ, stride=NC)
        recv_rows[g, pl.ds(0, NZ), :] = cells_ref[rows, :].astype(jnp.float32)
        recv_rows[g, pl.ds(NZ, NZ), :] = coef_ref[rows, :]

    def right_copy(r, i):
        part = pl.ds(2 * i, 2)
        return pltpu.make_async_remote_copy(
            src_ref=held.at[r, part], dst_ref=held.at[r + 1, part],
            send_sem=right_send.at[r, i], recv_sem=right_recv.at[r, i],
            device_id=near(dz=1), device_id_type=MESH)

    def left_copy(r, i):
        part = pl.ds(2 * i, 2)
        return pltpu.make_async_remote_copy(
            src_ref=held.at[(NZ - r) % NZ, part], dst_ref=held.at[NZ - r - 1, part],
            send_sem=left_send.at[r, i], recv_sem=left_recv.at[r, i],
            device_id=near(dz=-1), device_id_type=MESH)

    def list_copy(side, r):
        far = (SUBS, SUBS - 1)[side]
        part = pl.ds(r, far - r)
        return pltpu.make_async_remote_copy(
            src_ref=lists.at[side, r, part], dst_ref=lists.at[side, r + 1, part],
            send_sem=list_send.at[side, r], recv_sem=list_recv.at[side, r],
            device_id=near(dz=1 - 2 * side), device_id_type=MESH)

    def tell(n):
        for other in flow_near:
            pl.semaphore_signal(rounds.at[n], inc=1, device_id=other, device_id_type=MESH)

    def xmeta_copy(dx, dc):
        to_x, to_c = lax.rem(x + NX - dx, NX), lax.rem(c + dc, NC)
        return pltpu.make_async_remote_copy(
            src_ref=recv_rows.at[to_x * NC + to_c], dst_ref=xmeta.at[dx * NC + dc],
            send_sem=xm_send.at[dx * NC + dc], recv_sem=xm_recv.at[dx * NC + dc],
            device_id=peer(to_x, z, to_c), device_id_type=MESH)

    def pair_copy(dx, q):
        part = pl.ds(2 * q, 2)
        return pltpu.make_async_remote_copy(
            src_ref=to_partner.at[dx, part], dst_ref=from_partner.at[dx, part],
            send_sem=pair_send.at[dx, q], recv_sem=pair_recv.at[dx, q],
            device_id=near(dc=1), device_id_type=MESH)

    def relay_copy(q):
        return pltpu.make_async_remote_copy(
            src_ref=comb.at[2, pl.ds(2 * q, 2)], dst_ref=relay.at[q],
            send_sem=relay_send.at[q], recv_sem=relay_recv.at[q],
            device_id=near(dx=1 if q < 2 else -1), device_id_type=MESH)

    def final_copy(side, q):
        part = pl.ds(2 * q, 2)
        return pltpu.make_async_remote_copy(
            src_ref=comb.at[1 + 2 * side, part], dst_ref=final.at[side, part],
            send_sem=final_send.at[side, q], recv_sem=final_recv.at[side, q],
            device_id=near(dx=1 - 2 * side), device_id_type=MESH)

    def above_copy(k):
        return pltpu.make_async_remote_copy(
            src_ref=outlet, dst_ref=above.at[k - 1],
            send_sem=above_send.at[k - 1], recv_sem=above_recv.at[k - 1],
            device_id={"flow": lax.rem(flow + k, N_FLOW)}, device_id_type=MESH)

    def pass_copy(k):
        return pltpu.make_async_remote_copy(
            src_ref=passing, dst_ref=passages.at[k - 1],
            send_sem=pass_send.at[k - 1], recv_sem=pass_recv.at[k - 1],
            device_id={"flow": lax.rem(flow + k, N_FLOW)}, device_id_type=MESH)

    def response_start():
        resp[0] = jnp.zeros((CELLS + B, 2 * B), jnp.bfloat16)
        resp[0, pl.ds(CELLS, B), :] = beside(product(beside(flux_ref[0]), inverse_ref[0]))
        resp[0, pl.ds(0, B), :] = beside(inverse_ref[0])

    def response_step(j):
        inverse = inverse_ref[j]
        step = product(beside(flux_ref[j]), inverse)
        resp[j] = beside(product(resp[feeders[j]], step))
        resp[j, pl.ds(pl.multiple_of(j * B, B), B), :] = beside(inverse)

    def load_lhs(r, which):
        for b in range(NB):
            high, low = split(held[r, b])
            lhs[which, pl.ds(0, E), pl.ds(b * B, B)] = high
            lhs[which, pl.ds(E, E), pl.ds(b * B, B)] = low

    def pick(r, which, p):
        at = lax.rem(x + p, NX) * NC
        if r == 0:
            asked = send_rows.at[z]
        elif r <= SUBS:
            asked = lists.at[0, r, r - 1]
        else:
            asked = lists.at[1, NZ - r, NZ - r - 1]
        row = jnp.concatenate(
            [asked[pl.ds(at + lax.rem(c + dc, NC), 1), :] for dc in range(NC)], axis=1)
        zs = NZ + lax.rem(z + NZ - r, NZ)
        coef = jnp.concatenate(
            [xmeta[p * NC + dc, pl.ds(zs, 1), :] for dc in range(NC)], axis=1)
        choice = jnp.concatenate([one_hot(row, float(WIDE * q), iota_ref) for q in range(SUBS)], axis=0)
        both = dot(lhs[which], choice)
        value = (both[:E] + both[E:]) * coef
        high, low = split(value)
        t, half = WHERE[r]
        lanes = pl.ds(half * B, B)
        for dc in range(NC):
            weighted[p * NC + dc, t, pl.ds(0, E), lanes] = high[:, dc * B:(dc + 1) * B]
            weighted[p * NC + dc, t, pl.ds(E, E), lanes] = low[:, dc * B:(dc + 1) * B]

    def deposit(p, dc, t, q):
        put = to_partner if dc else comb
        landing = one_hot(xrow[p * NC + dc, t], float(WIDE * q), iota_ref)
        both = lax.dot_general(weighted[p * NC + dc, t], landing, (((1,), (1,)), ((), ())),
                               preferred_element_type=jnp.float32)
        value = both[:E] + both[E:]
        for i in range(2):
            piece = value[:, i * B:(i + 1) * B]
            put[p, 2 * q + i] = piece if t == 0 else put[p, 2 * q + i] + piece

    def deposit_all(p, t):
        for q in range(SUBS):
            for dc in range(NC):
                deposit(p, dc, t, q)

    pl.semaphore_wait(barrier, len(greeted))
    for i in range(SUBS):
        right_copy(0, i).start()
        left_copy(0, i).start()
        if i == 0:
            list_copy(0, 0).start()
            list_copy(1, 0).start()
            for dx, dc in group[1:]:
                xmeta_copy(dx, dc).start()
    tell(0)
    for load in loads[5:]:
        load.wait()
    xmeta[0] = recv_rows[x * NC + c]
    response_start()
    load_lhs(0, 0)
    for dx, dc in group[1:]:
        xmeta_copy(dx, dc).wait_recv()
    for d in range(GROUP):
        for r in range(NZ):
            t, half = WHERE[r]
            xrow[d, t, :, pl.ds(half * B, B)] = xmeta[d, pl.ds(lax.rem(z + NZ - r, NZ), 1), :]

    pl.semaphore_wait(rounds.at[0], 2)
    tell(1)

    for r in range(1, 4):
        for side in range(2):
            list_copy(side, r - 1).wait_recv()
            if r < (SUBS, SUBS - 1)[side]:
                list_copy(side, r).start()
        if r > 1:
            load_lhs(r - 1, 0)
            load_lhs(NZ - r + 1, 1)

        def ring(i, carry, r=r):
            right_copy(r - 1, i).wait_recv()
            if r < 3:
                right_copy(r, i).start()
            else:
                @pl.when(i < 2)
                def _():
                    right_copy(r, i).start()
            left_copy(r - 1, i).wait_recv()
            if r < 3:
                left_copy(r, i).start()
            else:
                @pl.when(i >= 2)
                def _():
                    left_copy(r, i).start()
            if r == 1:
                response_step(2 * i + 1)

                @pl.when(i < SUBS - 1)
                def _():
                    response_step(2 * i + 2)
                pick(0, 0, i)
            else:
                pick(r - 1, 0, i)
                pick(NZ - r + 1, 1, i)
                deposit_all(i, r - 2)
            return carry

        lax.fori_loop(0, SUBS, ring, 0)
        if r == 1:
            passing[...] = (resp[NB - 1, pl.ds(CELLS, B), pl.ds(0, B)].astype(jnp.float32)
                            + resp[NB - 1, pl.ds(CELLS, B), pl.ds(B, B)].astype(jnp.float32))
            pl.semaphore_wait(rounds.at[1], 2)
            tell(2)
        if r == 2:
            pl.semaphore_wait(rounds.at[2], 2)
            for k in range(1, N_FLOW - 1):
                @pl.when((flow >= 1) & (flow + k < N_FLOW))
                def _(k=k):
                    pass_copy(k).start()

    list_copy(0, 3).wait_recv()
    load_lhs(3, 0)
    load_lhs(5, 1)

    def late(p, carry):
        pick(3, 0, p)
        pick(5, 1, p)
        deposit_all(p, 2)
        return carry

    lax.fori_loop(0, SUBS, late, 0)
    for i in range(2):
        right_copy(3, i).wait_recv()
        left_copy(3, i + 2).wait_recv()
    load_lhs(4, 0)

    def finish(p, q):
        deposit(p, 1, 3, q)
        pair_copy(p, q).start()
        deposit(p, 0, 3, q)

    def combine(p, q):
        pair_copy(p, q).wait_recv()
        part = pl.ds(2 * q, 2)
        comb[p, part] = comb[p, part] + from_partner[p, part]

    pick(4, 0, 2)
    for q in range(SUBS):
        finish(2, q)
    pick(4, 0, 1)
    pick(4, 0, 3)
    for q in (0, 2, 1, 3):
        combine(2, q)
        relay_copy(q).start()
    early = ((0, 2), (1, 0), (0, 3), (1, 1))
    later = ((0, 0), (1, 2), (0, 1), (1, 3))
    for side, q in early:
        finish(1 + 2 * side, q)
    for side, q in early:
        combine(1 + 2 * side, q)
        final_copy(side, q).start()
    for side, q in later:
        finish(1 + 2 * side, q)
    for side, q in later:
        combine(1 + 2 * side, q)
    pick(4, 0, 0)
    for q in range(SUBS):
        finish(0, q)
    for side, q in later:
        relay_copy(q).wait_recv()
        part = pl.ds(2 * q, 2)
        comb[1 + 2 * side, part] = comb[1 + 2 * side, part] + relay[q]
        final_copy(side, q).start()
    for q in range(SUBS):
        combine(0, q)
    comb[0] = comb[0] + held[0]

    for k in range(1, N_FLOW - 1):
        @pl.when(flow > k)
        def _(k=k):
            pass_copy(k).wait_recv()
    two, four, six = (product(beside(passages[2 * i + 1]), passages[2 * i]) for i in range(3))
    whole_five, scale_five = scaled_rows(passages[4])
    whole_six, scale_six = scaled_rows(six)
    upper = product(beside(jnp.concatenate([whole_five, whole_six], axis=0)), four)
    whole_three, scale_three = scaled_rows(passages[2])
    whole_four, scale_four = scaled_rows(four)
    upper_five, more_five = scaled_rows(upper[:B])
    upper_six, more_six = scaled_rows(upper[B:])
    longer = product(beside(jnp.concatenate([whole_three, whole_four, upper_five, upper_six], axis=0)), two)
    chain[pl.ds(0, B), :] = beside(passages[0])
    chain[pl.ds(B, B), :] = beside(two)
    chain[pl.ds(2 * B, 4 * B), :] = beside(longer)
    ones = jnp.ones((1, B), jnp.float32)
    for k, (first, second) in enumerate((
            (ones, ones), (ones, ones), (scale_three, ones), (scale_four, ones),
            (scale_five, more_five), (scale_six, more_six))):
        chain_scale[k, pl.ds(0, 1), :] = first
        chain_scale[k, pl.ds(1, 1), :] = second

    for side, q in early:
        final_copy(side, q).wait_recv()
        part = pl.ds(2 * q, 2)
        comb[0, part] = comb[0, part] + final[side, part]
    for side, q in later:
        final_copy(side, q).wait_recv()
        for b in (2 * q, 2 * q + 1):
            high, low = split(comb[0, b] + final[side, b])
            src[pl.ds(0, E), pl.ds(b * B, B)] = high
            src[pl.ds(E, E), pl.ds(b * B, B)] = low

    def solve(j):
        return corners(dot(src[...], resp[j, pl.ds(0, CELLS), :]))

    outlet[...] = solve(NB - 1)
    for k in (4, 3, 5, 2, 6, 1, 7):
        @pl.when(flow + k < N_FLOW)
        def _(k=k):
            above_copy(k).start()
    settled_ref[:, NB - 1, :] = outlet[...]
    for j in range(NB - 1):
        settled_ref[:, j, :] = solve(j)

    for k in (7, 6, 5, 4, 3, 2, 1):
        @pl.when(flow >= k)
        def _(k=k):
            above_copy(k).wait_recv()
        if k > 1:
            high, low = split(above[k - 1] * chain_scale[k - 2, pl.ds(0, 1), :] * chain_scale[k - 2, pl.ds(1, 1), :])
            arriving[pl.ds(0, E), pl.ds((k - 2) * B, B)] = high
            arriving[pl.ds(E, E), pl.ds((k - 2) * B, B)] = low
    inflow = above[0] + corners(dot(arriving[...], chain[...]))
    parts = jnp.concatenate(split(inflow), axis=0)
    for j in range(NB):
        entered_ref[:, j, :] = corners(dot(parts, resp[j, pl.ds(CELLS, B), :]))

    for side in range(2):
        for r in range((SUBS, SUBS - 1)[side]):
            list_copy(side, r).wait_send()
    for dx, dc in group[1:]:
        xmeta_copy(dx, dc).wait_send()
    for r in range(3):
        for i in range(SUBS):
            right_copy(r, i).wait_send()
            left_copy(r, i).wait_send()
    for i in range(2):
        right_copy(3, i).wait_send()
        left_copy(3, i + 2).wait_send()
    for q in range(SUBS):
        for dx in range(NX):
            pair_copy(dx, q).wait_send()
        relay_copy(q).wait_send()
        for side in range(2):
            final_copy(side, q).wait_send()
    for k in range(1, N_FLOW):
        @pl.when(flow + k < N_FLOW)
        def _(k=k):
            above_copy(k).wait_send()
    for k in range(1, N_FLOW - 1):
        @pl.when((flow >= 1) & (flow + k < N_FLOW))
        def _(k=k):
            pass_copy(k).wait_send()


def step(feeders, counts, conc, couplings, inverses, send_cells, recv_cells, recv_coef):
    vmem = pl.BlockSpec(memory_space=pltpu.VMEM)
    f32, bf16, i32 = jnp.float32, jnp.bfloat16, jnp.int32
    dma = pltpu.SemaphoreType.DMA
    settled, entered = pl.pallas_call(
        step_kernel,
        out_shape=[jax.ShapeDtypeStruct((E, NB, B), f32)] * 2,
        in_specs=[pl.BlockSpec(memory_space=pl.ANY)] * 8,
        out_specs=[vmem, vmem],
        scratch_shapes=[
            pltpu.SMEM((NB,), i32),
            pltpu.SMEM((NZ * GROUP,), i32),
            pltpu.VMEM((E, NB, B), f32),
            pltpu.VMEM((NB, B, B), f32),
            pltpu.VMEM((NB, B, B), f32),
            pltpu.VMEM((NZ * GROUP, B), i32),
            pltpu.VMEM((NZ * GROUP, B), i32),
            pltpu.VMEM((NZ * GROUP, B), f32),
            pltpu.VMEM((NZ, NB, E, B), f32),
            pltpu.VMEM((2, 2 * E, CELLS), bf16),
            pltpu.VMEM((WIDE, WIDE), bf16),
            pltpu.VMEM((NZ, GROUP, B), f32),
            pltpu.VMEM((2, SUBS + 1, SUBS, GROUP, B), f32),
            pltpu.VMEM((GROUP, 2 * NZ, B), f32),
            pltpu.VMEM((GROUP, 2 * NZ, B), f32),
            pltpu.VMEM((GROUP, SUBS, 1, WIDE), f32),
            pltpu.VMEM((GROUP, SUBS, 2 * E, WIDE), bf16),
            pltpu.VMEM((NX, NB, E, B), f32),
            pltpu.VMEM((NX, NB, E, B), f32),
            pltpu.VMEM((NX, NB, E, B), f32),
            pltpu.VMEM((SUBS, 2, E, B), f32),
            pltpu.VMEM((2, NB, E, B), f32),
            pltpu.VMEM((NB, CELLS + B, 2 * B), bf16),
            pltpu.VMEM((2 * E, CELLS), bf16),
            pltpu.VMEM((E, B), f32),
            pltpu.VMEM((B, B), f32),
            pltpu.VMEM((N_FLOW - 1, E, B), f32),
            pltpu.VMEM((N_FLOW - 2, B, B), f32),
            pltpu.VMEM(((N_FLOW - 2) * B, 2 * B), bf16),
            pltpu.VMEM((N_FLOW - 2, 8, B), f32),
            pltpu.VMEM((2 * E, (N_FLOW - 2) * B), bf16),
            dma((8,)),
            dma((4, SUBS)), dma((4, SUBS)), dma((4, SUBS)), dma((4, SUBS)),
            dma((2, SUBS)), dma((2, SUBS)), dma((GROUP,)), dma((GROUP,)),
            dma((NX, SUBS)), dma((NX, SUBS)), dma((SUBS,)), dma((SUBS,)), dma((2, SUBS)), dma((2, SUBS)),
            dma((N_FLOW - 1,)), dma((N_FLOW - 1,)), dma((N_FLOW - 2,)), dma((N_FLOW - 2,)),
            pltpu.SemaphoreType.REGULAR((3,)),
        ],
        compiler_params=pltpu.CompilerParams(collective_id=0, has_side_effects=True),
        name="transport_step",
    )(feeders, counts, conc, couplings, inverses, send_cells, recv_cells, recv_coef)
    return settled + entered


def on_device(conc_old, face_flux, block_inverse, upstream_block, send_cells, send_count, recv_cells, recv_coef):
    return step(
        upstream_block[0, 0], send_count[0, 0], conc_old[0, 0], face_flux[0, 0], block_inverse[0, 0],
        send_cells[0, 0], recv_cells[0, 0], recv_coef[0, 0])[None, None]


def solution(mesh):
    placed = (
        P("flow", "cross", None, None, None),
        P("flow", "cross", None, None, None),
        P("flow", "cross", None, None, None),
        P("flow", "cross", None),
        P("flow", "cross", None, None),
        P("flow", "cross", None),
        P("flow", "cross", None, None),
        P("flow", "cross", None, None),
    )
    return jax.shard_map(
        on_device,
        mesh=mesh,
        in_specs=placed,
        out_specs=P("flow", "cross", None, None, None),
        check_vma=False,
    )
```

```python
import jax
import jax.numpy as jnp
from jax import lax
from jax.experimental import pallas as pl
from jax.experimental.pallas import tpu as pltpu
from jax.sharding import PartitionSpec as P

MESH = pl.DeviceIdType.MESH
E, NB, B = 64, 8, 128
CELLS = NB * B
N_FLOW = 8
NX, NZ, NC = 4, 8, 2
GROUP = NX * NC
SUBS = 4
WIDE = 256
ORDER = ((0, 1), (7, 2), (6, 3), (5, 4))
WHERE = {r: (t, half) for t, pair in enumerate(ORDER) for half, r in enumerate(pair)}


def split(value):
    high = value.astype(jnp.bfloat16)
    low = (value - high.astype(jnp.float32)).astype(jnp.bfloat16)
    return high, low


def dot(left, right):
    return jnp.dot(left, right, preferred_element_type=jnp.float32)


def beside(value):
    return jnp.concatenate(split(value), axis=1)


def product(left, right):
    high, low = split(right)
    whole = jnp.concatenate([jnp.concatenate([high, low], axis=1),
                             jnp.concatenate([high, jnp.zeros_like(low)], axis=1)], axis=0)
    both = dot(left, whole)
    return both[:, :B] + both[:, B:]


def corners(both):
    return both[:E, :B] + both[E:, :B] + both[:E, B:]


def one_hot(row, first, iota_ref):
    shifted = row - first
    inside = (shifted >= 0.0) & (shifted < float(WIDE))
    place = jnp.where(inside, shifted, -1.0).astype(jnp.bfloat16)
    hit = jnp.broadcast_to(place, (WIDE, WIDE)) == iota_ref[...]
    return jnp.where(hit, jnp.bfloat16(1), jnp.bfloat16(0))


def scaled_rows(matrix):
    top = jnp.maximum(jnp.max(matrix, axis=1, keepdims=True), 1e-30)
    column = jnp.broadcast_to(top, (B, B))
    return matrix / column, jnp.transpose(column)[0:1, :]


def step_kernel(feeders_in, counts_in, conc_in, flux_in, inverse_in, send_in, cells_in, coef_in,
                settled_ref, entered_ref,
                feeders, counts, conc_ref, flux_ref, inverse_ref, send_ref, cells_ref, coef_ref,
                held, lhs, iota_ref, send_rows, lists, recv_rows, xmeta, xrow, weighted,
                to_partner, from_partner, comb, relay, final,
                resp, src, outlet, passing, above, passages,
                chain, chain_scale, arriving,
                load_sem,
                right_send, right_recv, left_send, left_recv,
                list_send, list_recv, xm_send, xm_recv,
                pair_send, pair_recv, relay_send, relay_recv, final_send, final_recv,
                above_send, above_recv, pass_send, pass_recv, rounds):
    flow = lax.axis_index("flow")
    cross = lax.axis_index("cross")
    x = cross // (NZ * NC)
    z = lax.rem(cross // NC, NZ)
    c = lax.rem(cross, NC)

    def peer(px, pz, pc):
        return {"cross": (px * NZ + pz) * NC + pc}

    def near(dx=0, dz=0, dc=0):
        return peer(lax.rem(x + dx + NX, NX), lax.rem(z + dz + NZ, NZ), lax.rem(c + dc, NC))

    group = [(dx, dc) for dx in range(NX) for dc in range(NC)]

    barrier = pltpu.get_barrier_semaphore()
    flow_near = [{"flow": lax.rem(flow + k, N_FLOW)} for k in (1, N_FLOW - 1)]
    greeted = [near(dz=1), near(dz=-1)] + [near(dx=dx, dc=dc) for dx, dc in group[1:]] + flow_near
    for other in greeted:
        pl.semaphore_signal(barrier, inc=1, device_id=other, device_id_type=MESH)

    loads = [pltpu.make_async_copy(a, b, load_sem.at[i]) for i, (a, b) in enumerate((
        (conc_in, conc_ref), (counts_in, counts), (send_in, send_ref), (cells_in, cells_ref),
        (coef_in, coef_ref), (feeders_in, feeders), (flux_in, flux_ref), (inverse_in, inverse_ref)))]
    for load in loads:
        load.start()
    iota_ref[...] = lax.broadcasted_iota(jnp.int32, (WIDE, WIDE), 0).astype(jnp.float32).astype(jnp.bfloat16)
    for k in range(1, N_FLOW):
        @pl.when(flow < k)
        def _(k=k):
            above[k - 1] = jnp.zeros((E, B), jnp.float32)
    for k in range(1, N_FLOW - 1):
        @pl.when(flow <= k)
        def _(k=k):
            passages[k - 1] = jnp.zeros((B, B), jnp.float32)
    loads[0].wait()
    for b in range(NB):
        held[0, b] = conc_ref[:, b, :]

    def right_copy(r, i):
        part = pl.ds(2 * i, 2)
        return pltpu.make_async_remote_copy(
            src_ref=held.at[r, part], dst_ref=held.at[r + 1, part],
            send_sem=right_send.at[r, i], recv_sem=right_recv.at[r, i],
            device_id=near(dz=1), device_id_type=MESH)

    def left_copy(r, i):
        part = pl.ds(2 * i, 2)
        return pltpu.make_async_remote_copy(
            src_ref=held.at[(NZ - r) % NZ, part], dst_ref=held.at[NZ - r - 1, part],
            send_sem=left_send.at[r, i], recv_sem=left_recv.at[r, i],
            device_id=near(dz=-1), device_id_type=MESH)

    def list_copy(side, r):
        far = (SUBS, SUBS - 1)[side]
        part = pl.ds(r, far - r)
        return pltpu.make_async_remote_copy(
            src_ref=lists.at[side, r, part], dst_ref=lists.at[side, r + 1, part],
            send_sem=list_send.at[side, r], recv_sem=list_recv.at[side, r],
            device_id=near(dz=1 - 2 * side), device_id_type=MESH)

    def tell(n):
        for other in flow_near:
            pl.semaphore_signal(rounds.at[n], inc=1, device_id=other, device_id_type=MESH)

    def xmeta_copy(dx, dc):
        to_x, to_c = lax.rem(x + NX - dx, NX), lax.rem(c + dc, NC)
        return pltpu.make_async_remote_copy(
            src_ref=recv_rows.at[to_x * NC + to_c], dst_ref=xmeta.at[dx * NC + dc],
            send_sem=xm_send.at[dx * NC + dc], recv_sem=xm_recv.at[dx * NC + dc],
            device_id=peer(to_x, z, to_c), device_id_type=MESH)

    def pair_copy(dx, q):
        part = pl.ds(2 * q, 2)
        return pltpu.make_async_remote_copy(
            src_ref=to_partner.at[dx, part], dst_ref=from_partner.at[dx, part],
            send_sem=pair_send.at[dx, q], recv_sem=pair_recv.at[dx, q],
            device_id=near(dc=1), device_id_type=MESH)

    def relay_copy(q):
        return pltpu.make_async_remote_copy(
            src_ref=comb.at[2, pl.ds(2 * q, 2)], dst_ref=relay.at[q],
            send_sem=relay_send.at[q], recv_sem=relay_recv.at[q],
            device_id=near(dx=1 if q < 2 else -1), device_id_type=MESH)

    def final_copy(side, q):
        part = pl.ds(2 * q, 2)
        return pltpu.make_async_remote_copy(
            src_ref=comb.at[1 + 2 * side, part], dst_ref=final.at[side, part],
            send_sem=final_send.at[side, q], recv_sem=final_recv.at[side, q],
            device_id=near(dx=1 - 2 * side), device_id_type=MESH)

    def above_copy(k):
        return pltpu.make_async_remote_copy(
            src_ref=outlet, dst_ref=above.at[k - 1],
            send_sem=above_send.at[k - 1], recv_sem=above_recv.at[k - 1],
            device_id={"flow": lax.rem(flow + k, N_FLOW)}, device_id_type=MESH)

    def pass_copy(k):
        return pltpu.make_async_remote_copy(
            src_ref=passing, dst_ref=passages.at[k - 1],
            send_sem=pass_send.at[k - 1], recv_sem=pass_recv.at[k - 1],
            device_id={"flow": lax.rem(flow + k, N_FLOW)}, device_id_type=MESH)

    def response_start():
        resp[0] = jnp.zeros((CELLS + B, 2 * B), jnp.bfloat16)
        resp[0, pl.ds(CELLS, B), :] = beside(product(beside(flux_ref[0]), inverse_ref[0]))
        resp[0, pl.ds(0, B), :] = beside(inverse_ref[0])

    def response_step(j):
        inverse = inverse_ref[j]
        step = product(beside(flux_ref[j]), inverse)
        resp[j] = beside(product(resp[feeders[j]], step))
        resp[j, pl.ds(pl.multiple_of(j * B, B), B), :] = beside(inverse)

    def load_lhs(r, which):
        for b in range(NB):
            high, low = split(held[r, b])
            lhs[which, pl.ds(0, E), pl.ds(b * B, B)] = high
            lhs[which, pl.ds(E, E), pl.ds(b * B, B)] = low

    def pick(r, which, p):
        at = lax.rem(x + p, NX) * NC
        if r == 0:
            asked = send_rows.at[z]
        elif r <= SUBS:
            asked = lists.at[0, r, r - 1]
        else:
            asked = lists.at[1, NZ - r, NZ - r - 1]
        row = jnp.concatenate(
            [asked[pl.ds(at + lax.rem(c + dc, NC), 1), :] for dc in range(NC)], axis=1)
        zs = NZ + lax.rem(z + NZ - r, NZ)
        coef = jnp.concatenate(
            [xmeta[p * NC + dc, pl.ds(zs, 1), :] for dc in range(NC)], axis=1)
        choice = jnp.concatenate([one_hot(row, float(WIDE * q), iota_ref) for q in range(SUBS)], axis=0)
        both = dot(lhs[which], choice)
        value = (both[:E] + both[E:]) * coef
        high, low = split(value)
        t, half = WHERE[r]
        lanes = pl.ds(half * B, B)
        for dc in range(NC):
            weighted[p * NC + dc, t, pl.ds(0, E), lanes] = high[:, dc * B:(dc + 1) * B]
            weighted[p * NC + dc, t, pl.ds(E, E), lanes] = low[:, dc * B:(dc + 1) * B]

    def deposit(p, dc, t, q):
        put = to_partner if dc else comb
        landing = one_hot(xrow[p * NC + dc, t], float(WIDE * q), iota_ref)
        both = lax.dot_general(weighted[p * NC + dc, t], landing, (((1,), (1,)), ((), ())),
                               preferred_element_type=jnp.float32)
        value = both[:E] + both[E:]
        for i in range(2):
            piece = value[:, i * B:(i + 1) * B]
            put[p, 2 * q + i] = piece if t == 0 else put[p, 2 * q + i] + piece

    def deposit_all(p, t):
        for q in range(SUBS):
            for dc in range(NC):
                deposit(p, dc, t, q)

    pl.semaphore_wait(barrier, len(greeted))
    for i in range(SUBS):
        right_copy(0, i).start()
        left_copy(0, i).start()
    tell(0)
    for load in loads[1:5]:
        load.wait()
    lane = lax.broadcasted_iota(jnp.int32, (1, B), 1)
    for pz in range(NZ):
        for g in range(GROUP):
            peer_id = (g // NC) * NZ * NC + pz * NC + g % NC
            row = send_ref[pl.ds(peer_id, 1), :]
            live = jnp.where(lane < counts[peer_id], row, -1)
            send_rows[pz, pl.ds(g, 1), :] = live.astype(jnp.float32)
    for k in range(SUBS):
        lists[0, 0, k] = send_rows[lax.rem(z + k + 1, NZ)]
    for k in range(SUBS - 1):
        lists[1, 0, k] = send_rows[lax.rem(z + NZ - k - 1, NZ)]
    for g in range(GROUP):
        rows = pl.ds((g // NC) * NZ * NC + g % NC, NZ, stride=NC)
        recv_rows[g, pl.ds(0, NZ), :] = cells_ref[rows, :].astype(jnp.float32)
        recv_rows[g, pl.ds(NZ, NZ), :] = coef_ref[rows, :]
    list_copy(0, 0).start()
    list_copy(1, 0).start()
    for dx, dc in group[1:]:
        xmeta_copy(dx, dc).start()
    for load in loads[5:]:
        load.wait()
    xmeta[0] = recv_rows[x * NC + c]
    response_start()
    load_lhs(0, 0)
    for dx, dc in group[1:]:
        xmeta_copy(dx, dc).wait_recv()
    for d in range(GROUP):
        for r in range(NZ):
            t, half = WHERE[r]
            xrow[d, t, :, pl.ds(half * B, B)] = xmeta[d, pl.ds(lax.rem(z + NZ - r, NZ), 1), :]

    pl.semaphore_wait(rounds.at[0], 2)
    tell(1)

    for r in range(1, 4):
        for side in range(2):
            list_copy(side, r - 1).wait_recv()
            if r < (SUBS, SUBS - 1)[side]:
                list_copy(side, r).start()
        if r > 1:
            load_lhs(r - 1, 0)
            load_lhs(NZ - r + 1, 1)

        def ring(i, carry, r=r):
            right_copy(r - 1, i).wait_recv()
            if r < 3:
                right_copy(r, i).start()
            else:
                @pl.when(i < 2)
                def _():
                    right_copy(r, i).start()
            left_copy(r - 1, i).wait_recv()
            if r < 3:
                left_copy(r, i).start()
            else:
                @pl.when(i >= 2)
                def _():
                    left_copy(r, i).start()
            if r == 1:
                response_step(2 * i + 1)

                @pl.when(i < SUBS - 1)
                def _():
                    response_step(2 * i + 2)
                pick(0, 0, i)
            else:
                if r == 2:
                    @pl.when(i == 1)
                    def _():
                        pl.semaphore_wait(rounds.at[2], 2)
                    for k in range(1, N_FLOW - 1):
                        @pl.when((i == 1) & (flow >= 1) & (flow + k < N_FLOW))
                        def _(k=k):
                            pass_copy(k).start()
                pick(r - 1, 0, i)
                pick(NZ - r + 1, 1, i)
                deposit_all(i, r - 2)
            return carry

        lax.fori_loop(0, SUBS, ring, 0)
        if r == 1:
            passing[...] = (resp[NB - 1, pl.ds(CELLS, B), pl.ds(0, B)].astype(jnp.float32)
                            + resp[NB - 1, pl.ds(CELLS, B), pl.ds(B, B)].astype(jnp.float32))
            pl.semaphore_wait(rounds.at[1], 2)
            tell(2)

    list_copy(0, 3).wait_recv()
    load_lhs(3, 0)
    load_lhs(5, 1)

    def late(p, carry):
        pick(3, 0, p)
        pick(5, 1, p)
        return carry

    lax.fori_loop(0, SUBS, late, 0)
    deposit_all(2, 2)
    for i in range(2):
        right_copy(3, i).wait_recv()
        left_copy(3, i + 2).wait_recv()
    load_lhs(4, 0)

    def finish(p, q):
        left_over = (3,) if p == 2 else (2, 3)
        for t in left_over:
            deposit(p, 1, t, q)
        pair_copy(p, q).start()
        for t in left_over:
            deposit(p, 0, t, q)

    def combine(p, q):
        pair_copy(p, q).wait_recv()
        part = pl.ds(2 * q, 2)
        comb[p, part] = comb[p, part] + from_partner[p, part]

    pick(4, 0, 2)
    for q in range(SUBS):
        finish(2, q)
    pick(4, 0, 1)
    pick(4, 0, 3)
    for q in (0, 2, 1, 3):
        combine(2, q)
        relay_copy(q).start()
    early = ((0, 2), (1, 0), (0, 3), (1, 1))
    later = ((0, 0), (1, 2), (0, 1), (1, 3))
    for side, q in early:
        finish(1 + 2 * side, q)
    for side, q in early:
        combine(1 + 2 * side, q)
        final_copy(side, q).start()
    for side, q in later:
        finish(1 + 2 * side, q)
    for side, q in later:
        combine(1 + 2 * side, q)
    pick(4, 0, 0)
    for q in range(SUBS):
        finish(0, q)
    for side, q in later:
        relay_copy(q).wait_recv()
        part = pl.ds(2 * q, 2)
        comb[1 + 2 * side, part] = comb[1 + 2 * side, part] + relay[q]
        final_copy(side, q).start()
    for q in range(SUBS):
        combine(0, q)
    comb[0] = comb[0] + held[0]

    for k in range(1, N_FLOW - 1):
        @pl.when(flow > k)
        def _(k=k):
            pass_copy(k).wait_recv()
    two, four, six = (product(beside(passages[2 * i + 1]), passages[2 * i]) for i in range(3))
    whole_five, scale_five = scaled_rows(passages[4])
    whole_six, scale_six = scaled_rows(six)
    upper = product(beside(jnp.concatenate([whole_five, whole_six], axis=0)), four)
    whole_three, scale_three = scaled_rows(passages[2])
    whole_four, scale_four = scaled_rows(four)
    upper_five, more_five = scaled_rows(upper[:B])
    upper_six, more_six = scaled_rows(upper[B:])
    longer = product(beside(jnp.concatenate([whole_three, whole_four, upper_five, upper_six], axis=0)), two)
    chain[pl.ds(0, B), :] = beside(passages[0])
    chain[pl.ds(B, B), :] = beside(two)
    chain[pl.ds(2 * B, 4 * B), :] = beside(longer)
    ones = jnp.ones((1, B), jnp.float32)
    for k, (first, second) in enumerate((
            (ones, ones), (ones, ones), (scale_three, ones), (scale_four, ones),
            (scale_five, more_five), (scale_six, more_six))):
        chain_scale[k, pl.ds(0, 1), :] = first
        chain_scale[k, pl.ds(1, 1), :] = second

    for side, q in early:
        final_copy(side, q).wait_recv()
        part = pl.ds(2 * q, 2)
        comb[0, part] = comb[0, part] + final[side, part]
    for side, q in later:
        final_copy(side, q).wait_recv()
        for b in (2 * q, 2 * q + 1):
            high, low = split(comb[0, b] + final[side, b])
            src[pl.ds(0, E), pl.ds(b * B, B)] = high
            src[pl.ds(E, E), pl.ds(b * B, B)] = low

    def solve(j):
        return corners(dot(src[...], resp[j, pl.ds(0, CELLS), :]))

    outlet[...] = solve(NB - 1)
    for k in (4, 3, 5, 2, 6, 1, 7):
        @pl.when(flow + k < N_FLOW)
        def _(k=k):
            above_copy(k).start()
    settled_ref[:, NB - 1, :] = outlet[...]
    for j in range(NB - 1):
        settled_ref[:, j, :] = solve(j)

    for k in (7, 6, 5, 4, 3, 2, 1):
        @pl.when(flow >= k)
        def _(k=k):
            above_copy(k).wait_recv()
        if k > 1:
            high, low = split(above[k - 1] * chain_scale[k - 2, pl.ds(0, 1), :] * chain_scale[k - 2, pl.ds(1, 1), :])
            arriving[pl.ds(0, E), pl.ds((k - 2) * B, B)] = high
            arriving[pl.ds(E, E), pl.ds((k - 2) * B, B)] = low
    inflow = above[0] + corners(dot(arriving[...], chain[...]))
    parts = jnp.concatenate(split(inflow), axis=0)
    for j in range(NB):
        entered_ref[:, j, :] = corners(dot(parts, resp[j, pl.ds(CELLS, B), :]))

    for side in range(2):
        for r in range((SUBS, SUBS - 1)[side]):
            list_copy(side, r).wait_send()
    for dx, dc in group[1:]:
        xmeta_copy(dx, dc).wait_send()
    for r in range(3):
        for i in range(SUBS):
            right_copy(r, i).wait_send()
            left_copy(r, i).wait_send()
    for i in range(2):
        right_copy(3, i).wait_send()
        left_copy(3, i + 2).wait_send()
    for q in range(SUBS):
        for dx in range(NX):
            pair_copy(dx, q).wait_send()
        relay_copy(q).wait_send()
        for side in range(2):
            final_copy(side, q).wait_send()
    for k in range(1, N_FLOW):
        @pl.when(flow + k < N_FLOW)
        def _(k=k):
            above_copy(k).wait_send()
    for k in range(1, N_FLOW - 1):
        @pl.when((flow >= 1) & (flow + k < N_FLOW))
        def _(k=k):
            pass_copy(k).wait_send()


def step(feeders, counts, conc, couplings, inverses, send_cells, recv_cells, recv_coef):
    vmem = pl.BlockSpec(memory_space=pltpu.VMEM)
    f32, bf16, i32 = jnp.float32, jnp.bfloat16, jnp.int32
    dma = pltpu.SemaphoreType.DMA
    settled, entered = pl.pallas_call(
        step_kernel,
        out_shape=[jax.ShapeDtypeStruct((E, NB, B), f32)] * 2,
        in_specs=[pl.BlockSpec(memory_space=pl.ANY)] * 8,
        out_specs=[vmem, vmem],
        scratch_shapes=[
            pltpu.SMEM((NB,), i32),
            pltpu.SMEM((NZ * GROUP,), i32),
            pltpu.VMEM((E, NB, B), f32),
            pltpu.VMEM((NB, B, B), f32),
            pltpu.VMEM((NB, B, B), f32),
            pltpu.VMEM((NZ * GROUP, B), i32),
            pltpu.VMEM((NZ * GROUP, B), i32),
            pltpu.VMEM((NZ * GROUP, B), f32),
            pltpu.VMEM((NZ, NB, E, B), f32),
            pltpu.VMEM((2, 2 * E, CELLS), bf16),
            pltpu.VMEM((WIDE, WIDE), bf16),
            pltpu.VMEM((NZ, GROUP, B), f32),
            pltpu.VMEM((2, SUBS + 1, SUBS, GROUP, B), f32),
            pltpu.VMEM((GROUP, 2 * NZ, B), f32),
            pltpu.VMEM((GROUP, 2 * NZ, B), f32),
            pltpu.VMEM((GROUP, SUBS, 1, WIDE), f32),
            pltpu.VMEM((GROUP, SUBS, 2 * E, WIDE), bf16),
            pltpu.VMEM((NX, NB, E, B), f32),
            pltpu.VMEM((NX, NB, E, B), f32),
            pltpu.VMEM((NX, NB, E, B), f32),
            pltpu.VMEM((SUBS, 2, E, B), f32),
            pltpu.VMEM((2, NB, E, B), f32),
            pltpu.VMEM((NB, CELLS + B, 2 * B), bf16),
            pltpu.VMEM((2 * E, CELLS), bf16),
            pltpu.VMEM((E, B), f32),
            pltpu.VMEM((B, B), f32),
            pltpu.VMEM((N_FLOW - 1, E, B), f32),
            pltpu.VMEM((N_FLOW - 2, B, B), f32),
            pltpu.VMEM(((N_FLOW - 2) * B, 2 * B), bf16),
            pltpu.VMEM((N_FLOW - 2, 8, B), f32),
            pltpu.VMEM((2 * E, (N_FLOW - 2) * B), bf16),
            dma((8,)),
            dma((4, SUBS)), dma((4, SUBS)), dma((4, SUBS)), dma((4, SUBS)),
            dma((2, SUBS)), dma((2, SUBS)), dma((GROUP,)), dma((GROUP,)),
            dma((NX, SUBS)), dma((NX, SUBS)), dma((SUBS,)), dma((SUBS,)), dma((2, SUBS)), dma((2, SUBS)),
            dma((N_FLOW - 1,)), dma((N_FLOW - 1,)), dma((N_FLOW - 2,)), dma((N_FLOW - 2,)),
            pltpu.SemaphoreType.REGULAR((3,)),
        ],
        compiler_params=pltpu.CompilerParams(collective_id=0, has_side_effects=True),
        name="transport_step",
    )(feeders, counts, conc, couplings, inverses, send_cells, recv_cells, recv_coef)
    return settled + entered


def on_device(conc_old, face_flux, block_inverse, upstream_block, send_cells, send_count, recv_cells, recv_coef):
    return step(
        upstream_block[0, 0], send_count[0, 0], conc_old[0, 0], face_flux[0, 0], block_inverse[0, 0],
        send_cells[0, 0], recv_cells[0, 0], recv_coef[0, 0])[None, None]


def solution(mesh):
    placed = (
        P("flow", "cross", None, None, None),
        P("flow", "cross", None, None, None),
        P("flow", "cross", None, None, None),
        P("flow", "cross", None),
        P("flow", "cross", None, None),
        P("flow", "cross", None),
        P("flow", "cross", None, None),
        P("flow", "cross", None, None),
    )
    return jax.shard_map(
        on_device,
        mesh=mesh,
        in_specs=placed,
        out_specs=P("flow", "cross", None, None, None),
        check_vma=False,
    )
```
